32 devices in a mesh: frame: 8 (over z, y), head: 2 (over x), batch: 2 (over core).
Axes of the slice: x: 2, y: 2, z: 4, core: 2. Of those that a mesh axis runs over, the one named last changes fastest.
Arguments:
- tokens: bfloat16 [8192, 1536], P(('batch', 'frame')), parts along dimension 0, may hold values from -6 to 6
- query_weight: bfloat16 [1536, 1536], P(None, 'head'), may hold values from -0.15625 to 0.15625
- key_weight: bfloat16 [1536, 1536], P(None, 'head'), may hold values from -0.15625 to 0.15625
- value_weight: bfloat16 [1536, 1536], P(None, 'head'), may hold values from -0.15625 to 0.15625
- out_weight: bfloat16 [1536, 1536], P('head'), may hold values from -0.625 to 0.625
- block_mask: int32 [16, 4, 13], P(('batch', 'frame')), parts along dimension 0, may hold values from 0 to 1, as said below
- frame_level: int32 [64], P(('batch', 'frame')), parts along dimension 0, may hold values from 0 to 15
- modulation: float32 [16, 2, 1536], replicated, may hold values from -1.2 to 13
Outputs:
- layer_out: bfloat16 [8192, 1536], P(('batch', 'frame'), 'head'), parts along dimension 0
The draws below stay inside these ranges and needn't reach their ends.
There are 2 independent parts, one for each index of `batch`. The reference program is written for one: setup_inputs(seed, part) draws one part's arguments, and reference() takes and returns one part's arrays. A program takes and returns all parts, laid end to end along the dimension named above; an argument that names none is the same for every part. Nothing has to cross between parts.
Inputs may be any that keep to these rules, and one draw needn't show every extreme that they name: `block_mask`: in span c every tile with key block below 1, and the tile of query block i with key block (1152) / 128 + i, is always 1; the share of the other tiles that are 1 differs from span to span.
All inputs are finite; a program needn't handle non-finite values.
Results may differ from the reference program's by a relative error of at most 0.01.
The reference program's roundings to bfloat16 on the way count: a program that leaves them out, or rounds other values in their place, can miss the bound.
Values may be sent and summed in bfloat16 or wider, within the bound.
A program may use at most 128 MiB of HBM per device.

```python
import math
import jax
import jax.numpy as jnp
from jax import lax

D = 1536
HEADS = 12
HEAD_DIM = 128
SPAN = 512
FRAME_TOK = 128
SINK = 128
TILE = 128
LEVELS = 16
SPANS = 8
TOKENS = 4096
FRAMES = 32
KEYS = 1664
QBLOCKS = 4
KBLOCKS = 13


def draw_block_mask(key, part):
    first_key, second_key = jax.random.split(key)
    density = jax.random.randint(first_key, (SPANS, 1, 1), 3, 11)
    rolled = jax.random.randint(second_key, (SPANS, QBLOCKS, KBLOCKS), 0, 10)
    tile_bits = rolled < density
    diagonal = jnp.arange(KBLOCKS)[None, :] == (SINK + 2 * SPAN) // TILE + jnp.arange(QBLOCKS)[:, None]
    sink_cols = jnp.broadcast_to(jnp.arange(KBLOCKS)[None, :] < SINK // TILE, (QBLOCKS, KBLOCKS))
    return (tile_bits | diagonal[None] | sink_cols[None]).astype(jnp.int32)


def draw_modulation(key, part):
    first_key = jax.random.fold_in(key, 0)
    table_values = jnp.clip(0.3 * jax.random.normal(first_key, (LEVELS, 2, D), jnp.float32), -1.2, 1.2)
    return table_values.astype(jnp.float32)


def plant(result, rng, least, top_value):
    dims = result.shape
    index_at = [jax.random.randint(jax.random.fold_in(rng, axis), (), 0, dims[axis]) for axis in range(len(dims))]
    result = result.at[tuple(index_at)].set(least)
    longest = dims.index(max(dims))
    index_at[longest] = (index_at[longest] + 1) % dims[longest]
    return result.at[tuple(index_at)].set(top_value)


def levels(own_key, shape, cuts, smallest, top_value):
    level, own = 1.0, jax.random.fold_in(own_key, 6)
    for dim, shards_of in cuts:
        steps = jnp.exp(jax.random.uniform(jax.random.fold_in(own, dim), (shards_of,), jnp.float32, smallest / len(cuts), top_value / len(cuts)))
        level = level * jnp.repeat(steps, shape[dim] // shards_of).reshape([-1 if axis == dim else 1 for axis in range(len(shape))])
    return level


def bell_draw(stream_key, dims, deviation, reach, shards=(), kind=jnp.bfloat16):
    array = jax.random.normal(stream_key, dims, jnp.float32) * deviation
    if len(shards) > 0:
        array = levels(stream_key, dims, shards, -0.22, 0.18) * array
    return jnp.clip(array, min=-reach, max=reach).astype(kind)


def setup_inputs(seed: int = 0, part: int = 0) -> dict:
    splits = jax.random.split(jax.random.key(seed), 9)
    part_splits = jax.random.split(jax.random.fold_in(splits[8], part), 9)
    tokens = bell_draw(part_splits[0], (TOKENS, D), 1.0, 6.0, ((0, 8),))
    query_weight = bell_draw(splits[1], (D, D), D ** -0.5, 0.15625, ((1, 2),))
    key_weight = bell_draw(splits[2], (D, D), D ** -0.5, 0.15625, ((1, 2),))
    value_weight = bell_draw(splits[3], (D, D), D ** -0.5, 0.15625, ((1, 2),))
    out_weight = bell_draw(splits[4], (D, D), (D // 16) ** -0.5, 0.625, ((0, 2),))
    block_mask = draw_block_mask(jax.random.fold_in(jax.random.fold_in(splits[8], part), 71), part)
    frame_level = plant(jax.random.randint(part_splits[6], (FRAMES,), 0, LEVELS), jax.random.fold_in(part_splits[6], 1), 0, LEVELS - 1).astype(jnp.int32)
    modulation = draw_modulation(jax.random.fold_in(splits[8], 71), part)
    return {"tokens": tokens, "query_weight": query_weight, "key_weight": key_weight, "value_weight": value_weight, "out_weight": out_weight, "block_mask": block_mask, "frame_level": frame_level, "modulation": modulation}


def visible(span_index, span_len, total_keys):
    key_place = jnp.arange(total_keys, dtype=jnp.int32)
    near_start = SINK + span_len
    own_start = SINK + 2 * span_len
    return (key_place < SINK) | (key_place >= own_start) | (key_place >= near_start) & (span_index >= 1) | (key_place < near_start) & (span_index >= 2)

def reference(tokens, query_weight, key_weight, value_weight, out_weight, block_mask, frame_level, modulation):
    xfloat = tokens.astype(jnp.float32)
    mean_square = lax.optimization_barrier(jnp.mean(xfloat * xfloat, axis=-1, keepdims=True))
    normed = xfloat * lax.rsqrt(mean_square + 1e-06)
    chosen = modulation[frame_level]
    shaped = normed.reshape(FRAMES, FRAME_TOK, D)
    modulated = (shaped * (1.0 + chosen[:, None, 0]) + chosen[:, None, 1]).reshape(TOKENS, D).astype(jnp.bfloat16)
    score_scale = 1.0 / math.sqrt(HEAD_DIM)
    query_all = (jnp.dot(modulated, query_weight, preferred_element_type=jnp.float32) * score_scale).astype(jnp.bfloat16).reshape(SPANS, SPAN, HEADS, HEAD_DIM)
    key_all = jnp.dot(modulated, key_weight, preferred_element_type=jnp.float32).astype(jnp.bfloat16).reshape(SPANS, SPAN, HEADS, HEAD_DIM)
    value_all = jnp.dot(modulated, value_weight, preferred_element_type=jnp.float32).astype(jnp.bfloat16).reshape(SPANS, SPAN, HEADS, HEAD_DIM)
    sink_keys = key_all[0, :SINK]
    sink_values = value_all[0, :SINK]

    def one_span(span_index):
        earlier = jnp.maximum(span_index - 2, 0)
        previous = jnp.maximum(span_index - 1, 0)
        key_rows = jnp.concatenate([sink_keys, key_all[earlier], key_all[previous], key_all[span_index]], axis=0)
        value_rows = jnp.concatenate([sink_values, value_all[earlier], value_all[previous], value_all[span_index]], axis=0)
        tile_mask = block_mask[span_index]
        tile_full = jnp.broadcast_to(tile_mask[:, None, :, None], (QBLOCKS, TILE, KBLOCKS, TILE)).reshape(SPAN, KEYS)
        allowed = (tile_full > 0) & visible(span_index, SPAN, KEYS)[None, :]
        score_rows = jnp.einsum('qhd,khd->hqk', query_all[span_index].astype(jnp.float32), key_rows.astype(jnp.float32))
        masked_scores = jnp.where(allowed[None], score_rows, -1e+30)
        row_peak = lax.optimization_barrier(jnp.max(masked_scores, axis=-1, keepdims=True))
        softmax_num = jnp.where(allowed[None], jnp.exp(masked_scores - row_peak), 0.0)
        row_total = lax.optimization_barrier(jnp.sum(softmax_num, axis=-1))
        weights_bf = lax.optimization_barrier(softmax_num.astype(jnp.bfloat16))
        mixed_rows = jnp.einsum('hqk,khd->qhd', weights_bf.astype(jnp.float32), value_rows.astype(jnp.float32))
        return (mixed_rows / row_total.T[:, :, None]).astype(jnp.bfloat16).reshape(SPAN, D)
    attention_out = lax.map(one_span, jnp.arange(SPANS, dtype=jnp.int32)).reshape(TOKENS, D)
    return (xfloat + jnp.dot(attention_out, out_weight, preferred_element_type=jnp.float32)).astype(jnp.bfloat16)
```

```python
import functools
import math

import jax
import jax.numpy as jnp
from jax import lax
from jax.experimental import pallas as pl
from jax.experimental.pallas import tpu as pltpu
from jax.sharding import PartitionSpec as P

HEAD_DIM = 128
FRAME_TOK = 128
SINK = 128
TILE = 128
CHUNK = 32
DIRECT = 9
EARLY = 4
PIECE = 32
BLOCKED = -1e30
MESH = pl.DeviceIdType.MESH
BF16, F32 = jnp.bfloat16, jnp.float32


def layer_kernel(
    frames,
    tok_hbm,
    wq_hbm,
    wk_hbm,
    wv_hbm,
    wo_hbm,
    mask_ref,
    level_ref,
    table_ref,
    out_ref,
    tok,
    resid,
    wq,
    wk,
    wv,
    wo_mine,
    wo_theirs,
    own,
    near,
    sink,
    qbuf,
    kbuf,
    vbuf,
    qmark,
    kmark,
    ones,
    far_rule,
    their_rule,
    their_mark,
    their_q,
    their_out,
    their_lse,
    far_out,
    far_lse,
    peak_buf,
    total_buf,
    mixed_buf,
    outgoing,
    incoming,
    kept,
    load_sem,
    send_near,
    send_x,
    recv_near,
    send_sink,
    recv_sink,
    send_q,
    recv_q,
    send_rule,
    recv_rule,
    send_o,
    recv_o,
    send_l,
    recv_l,
    send_out,
    recv_out,
):
    c = lax.axis_index("frame")
    h = lax.axis_index("head")
    span, width = own.shape
    local = wq.shape[1]
    share = out_ref.shape[1]
    heads = local // HEAD_DIM
    blocks = span // TILE
    chunks = span // CHUNK
    relays = chunks - DIRECT
    half_rows = span // 2
    half_blocks = blocks // 2
    pieces = SINK // 2 // PIECE
    sink_at, first_at, last_at = span, span + SINK, span + SINK + half_rows
    keys_end = kbuf.shape[0]

    has_near, gives_near = c >= 1, c + 1 < frames
    has_far, serves = c >= 2, c + 2 < frames

    def load(src, dst, i):
        return pltpu.make_async_copy(src, dst, load_sem.at[i])

    my_cols = pl.ds(pl.multiple_of(h * share, share), share)
    their_cols = pl.ds(pl.multiple_of((1 - h) * share, share), share)
    loads = [
        load(tok_hbm, tok, 0),
        load(wq_hbm, wq, 1),
        load(wk_hbm, wk, 2),
        load(wv_hbm, wv, 3),
        load(wo_hbm.at[:, their_cols], wo_theirs, 4),
        load(wo_hbm.at[:, my_cols], wo_mine, 5),
        load(tok_hbm.at[:, my_cols], resid, 6),
    ]
    for one in loads:
        one.start()

    barrier = pltpu.get_barrier_semaphore()
    pl.semaphore_signal(barrier, inc=1, device_id={"head": 1 - h}, device_id_type=MESH)
    expected = 1
    for step in (1, 2):
        for there, valid in ((c - step, c >= step), (c + step, c + step < frames)):

            @pl.when(valid)
            def _():
                pl.semaphore_signal(
                    barrier, inc=1, device_id={"frame": there}, device_id_type=MESH
                )

            expected = expected + jnp.where(valid, 1, 0)

    def rule_rows(j, valid, count):
        lane = lax.broadcasted_iota(jnp.int32, (count, TILE), 1)
        row = jnp.zeros((count, TILE), F32)
        for i in range(blocks):
            seen = mask_ref[i, j]
            if valid is not None:
                seen = seen * jnp.where(valid, 1, 0)
            row = jnp.where(lane == i, jnp.where(seen > 0, 0.0, BLOCKED), row)
        return row.astype(BF16)

    lane_at = lax.broadcasted_iota(jnp.int32, (TILE, TILE), 1)
    for i in range(blocks):
        qmark[i * TILE : (i + 1) * TILE, :] = jnp.where(lane_at == i, 1.0, 0.0).astype(BF16)
    near_tile, own_tile = (SINK + span) // TILE, (SINK + 2 * span) // TILE
    key_tiles = [own_tile + j for j in range(blocks)] + [0]
    key_tiles += [near_tile, near_tile + blocks - 1]
    key_tiles += [near_tile + j for j in range(1, blocks - 1)]
    for place_at, j in enumerate(key_tiles):
        valid = has_near if near_tile <= j < own_tile else None
        kmark[place_at * TILE : (place_at + 1) * TILE, :] = rule_rows(j, valid, TILE)
    for j in range(blocks):
        far_rule[j * 16 : (j + 1) * 16, :] = rule_rows(SINK // TILE + j, None, 16)
    ones[...] = jnp.ones(ones.shape, BF16)

    pl.semaphore_wait(barrier, expected)

    def remote(src, dst, send, recv, device):
        return pltpu.make_async_remote_copy(
            src_ref=src,
            dst_ref=dst,
            send_sem=send,
            recv_sem=recv,
            device_id=device,
            device_id_type=MESH,
        )

    def place(k):
        return jnp.where(h == 0, k, chunks - 1 - k)

    def other_place(k):
        return jnp.where(h == 0, chunks - 1 - k, k)

    def chunk_rows(i):
        return pl.ds(pl.multiple_of(i * CHUNK, CHUNK), CHUNK)

    def near_copy(k):
        at = chunk_rows(place(k))
        return remote(
            own.at[at], near.at[at], send_near.at[k], recv_near.at[place(k)], {"frame": c + 1}
        )

    def x_copy(k):
        at = chunk_rows(place(k))
        return remote(
            near.at[at], near.at[at], send_x.at[k], recv_near.at[place(k)], {"head": 1 - h}
        )

    def x_arrival(k):
        at = chunk_rows(other_place(k))
        return remote(
            near.at[at], near.at[at], send_x.at[k], recv_near.at[other_place(k)], {"head": 1 - h}
        )

    def sink_copy(p, n, device, half):
        at = pl.ds(pl.multiple_of((half * pieces + p) * PIECE, PIECE), PIECE)
        return remote(
            sink.at[at],
            sink.at[at],
            send_sink.at[n * pieces + p],
            recv_sink.at[half * pieces + p],
            device,
        )

    def sink_z(p):
        return sink_copy(p, 0, {"frame": c + 2}, h)

    def sink_y(p):
        return sink_copy(p, 1, {"frame": c + 1}, h)

    def sink_x(p, half):
        return sink_copy(p, 2, {"head": 1 - h}, half)

    def block_rows(b):
        return pl.ds(pl.multiple_of(b * TILE, TILE), TILE)

    def q_copy(b):
        at = block_rows(b)
        return remote(qbuf.at[at], their_q.at[at], send_q.at[b], recv_q.at[b], {"frame": c - 2})

    def rule_copy():
        return remote(far_rule, their_rule, send_rule.at[0], recv_rule.at[0], {"frame": c - 2})

    def o_copy(b):
        at = block_rows(b)
        return remote(their_out.at[at], far_out.at[at], send_o.at[b], recv_o.at[b], {"frame": c + 2})

    def l_copy(b):
        return remote(
            their_lse.at[b, pl.ds(0, 8)],
            far_lse.at[b, pl.ds(0, 8)],
            send_l.at[b],
            recv_l.at[b],
            {"frame": c + 2},
        )

    def out_copy(b):
        return remote(outgoing.at[b], incoming.at[b], send_out.at[b], recv_out.at[b], {"head": 1 - h})

    def modulate(start, count):
        x = tok[pl.ds(start, count), :].astype(F32)
        mean_square = jnp.mean(x * x, axis=-1, keepdims=True)
        normed = x * lax.rsqrt(mean_square + 1e-06)
        scale_shift = table_ref[level_ref[start // FRAME_TOK]]
        return (normed * (1.0 + scale_shift[0:1]) + scale_shift[1:2]).astype(BF16)

    loads[0].wait()

    @pl.when(c == 0)
    def _():
        for i in range(SINK // PIECE):
            sink[i * PIECE : (i + 1) * PIECE, :] = modulate(i * PIECE, PIECE)
        for p in range(pieces):
            sink_y(p).start()

            @pl.when(serves)
            def _():
                sink_z(p).start()

    def direct(k, carry):
        start = pl.multiple_of(place(k) * CHUNK, CHUNK)
        own[pl.ds(start, CHUNK), :] = modulate(start, CHUNK)

        @pl.when(gives_near)
        def _():
            near_copy(k).start()

        return carry

    lax.fori_loop(0, DIRECT, direct, 0)

    def rest(k, carry):
        start = pl.multiple_of(place(k) * CHUNK, CHUNK)
        own[pl.ds(start, CHUNK), :] = modulate(start, CHUNK)
        return carry

    lax.fori_loop(DIRECT, chunks, rest, 0)

    def project(flat, weight, dst, start, scale=None):
        res = jnp.dot(flat, weight[...], preferred_element_type=F32)
        if scale is not None:
            res = res * scale
        dst[start : start + flat.shape[0], :] = res.astype(BF16)

    def near_relay(k):
        @pl.when(has_near)
        def _():
            near_copy(k).wait_recv()
            if k < relays:
                x_copy(k).start()

    def sink_relay(lo, hi):
        @pl.when((c >= lo) & (c < hi))
        def _():
            for p in range(pieces):
                sink_z(p).wait_recv()
                sink_x(p, h).start()

                @pl.when(serves)
                def _():
                    sink_z(p).start()

    def head_cols(n):
        return slice(n * HEAD_DIM, (n + 1) * HEAD_DIM)

    def score(q_ref, q_at, q_stop, k_at, k_stop, mark, mark_at, n):
        left = jnp.concatenate([q_ref[q_at:q_stop, head_cols(n)], qmark[q_at:q_stop, :]], axis=1)
        marks = mark[mark_at : mark_at + k_stop - k_at, :]
        right = jnp.concatenate([kbuf[k_at:k_stop, head_cols(n)], marks], axis=1)
        return lax.dot_general(left, right, (((1,), (1,)), ((), ())), preferred_element_type=F32)

    def mix(num, k_at, k_stop, n):
        right = jnp.concatenate(
            [vbuf[k_at:k_stop, head_cols(n)], ones[0 : k_stop - k_at, :]], axis=1
        )
        both = jnp.dot(num.astype(BF16), right, preferred_element_type=F32)
        return both[:, :HEAD_DIM], both[:, HEAD_DIM:]

    def wide(column, shape):
        return jnp.broadcast_to(column, shape)

    loads[1].wait()
    project(own[...], wq, qbuf, 0, 1.0 / math.sqrt(HEAD_DIM))

    @pl.when(has_far)
    def _():
        rule_copy().start()
        for b in range(blocks):
            q_copy(b).start()

    near_relay(0)
    loads[2].wait()
    project(own[...], wk, kbuf, 0)
    loads[3].wait()
    project(own[...], wv, vbuf, 0)

    sink_relay(1, 4)
    near_relay(1)

    for n in range(heads):
        scores = score(qbuf, 0, span, 0, span, kmark, 0, n)
        peak = jnp.max(scores, axis=-1, keepdims=True)
        rows_out, total = mix(jnp.exp(scores - peak), 0, span, n)
        peak_buf[:, head_cols(n)] = wide(peak, total.shape)
        total_buf[:, head_cols(n)] = total
        mixed_buf[:, head_cols(n)] = rows_out

    near_relay(2)
    sink_relay(4, 6)
    near_relay(3)
    sink_relay(6, frames)

    @pl.when(has_near)
    def _():
        for k in range(EARLY):
            x_arrival(k).wait_recv()
        flat = jnp.concatenate([near[0:TILE, :], near[span - TILE : span, :]], axis=0)
        project(flat, wk, kbuf, first_at)
        project(flat, wv, vbuf, first_at)

    @pl.when(jnp.logical_not(has_near))
    def _():
        kbuf[first_at:keys_end, :] = jnp.zeros((keys_end - first_at, local), BF16)
        vbuf[first_at:keys_end, :] = jnp.zeros((keys_end - first_at, local), BF16)

    near_relay(4)

    def serve(g):
        lo, hi = g * half_rows, (g + 1) * half_rows

        @pl.when(serves)
        def _():
            if g == 0:
                rule_copy().wait_recv()
                for j in range(blocks):
                    small = their_rule[j * 16 : (j + 1) * 16, :]
                    their_mark[j * TILE : (j + 1) * TILE, :] = jnp.concatenate(
                        [small] * (TILE // 16), axis=0
                    )
            for b in range(g * half_blocks, (g + 1) * half_blocks):
                q_copy(b).wait_recv()
            lanes = lax.broadcasted_iota(jnp.int32, (half_rows, HEAD_DIM), 1)
            lse_all = jnp.zeros((half_rows, HEAD_DIM), F32)
            for n in range(heads):
                scores = score(their_q, lo, hi, 0, span, their_mark, 0, n)
                peak = jnp.max(scores, axis=-1, keepdims=True)
                rows_out, total = mix(jnp.exp(scores - peak), 0, span, n)
                their_out[lo:hi, head_cols(n)] = (rows_out / total).astype(BF16)
                lse_all = jnp.where(lanes == n, peak + jnp.log(total), lse_all)
            for b in range(half_blocks):
                their_lse[g * half_blocks + b] = lse_all[b * TILE : (b + 1) * TILE, :].T
            for b in range(g * half_blocks, (g + 1) * half_blocks):
                l_copy(b).start()
                o_copy(b).start()

    serve(0)
    near_relay(5)
    near_relay(6)

    @pl.when(has_near)
    def _():
        for p in range(pieces):
            sink_x(p, 1 - h).wait_recv()

    project(sink[...], wk, kbuf, sink_at)
    project(sink[...], wv, vbuf, sink_at)

    for n in range(heads):
        scores = score(qbuf, 0, span, sink_at, last_at, kmark, sink_at, n)
        before = peak_buf[:, head_cols(n)]
        peak = jnp.maximum(jnp.max(scores, axis=-1, keepdims=True), before)
        keep = jnp.exp(before - peak)
        spread = jnp.concatenate([peak] * (scores.shape[1] // HEAD_DIM), axis=1)
        rows_out, total = mix(jnp.exp(scores - spread), sink_at, last_at, n)
        peak_buf[:, head_cols(n)] = peak
        total_buf[:, head_cols(n)] = total_buf[:, head_cols(n)] * keep + total
        mixed_buf[:, head_cols(n)] = mixed_buf[:, head_cols(n)] * keep + rows_out

    for i in (4, 5, 6):
        loads[i].wait()

    @pl.when(has_near)
    def _():
        for k in range(relays, DIRECT):
            near_copy(k).wait_recv()
        for k in range(EARLY, relays):
            x_arrival(k).wait_recv()
        flat = near[TILE : span - TILE, :]
        project(flat, wk, kbuf, last_at)
        project(flat, wv, vbuf, last_at)

    @pl.when(jnp.logical_not(has_far))
    def _():
        far_out[...] = jnp.zeros(far_out.shape, BF16)
        far_lse[...] = jnp.full(far_lse.shape, BLOCKED, F32)

    def attend(g):
        lo, hi = g * half_rows, (g + 1) * half_rows

        @pl.when(has_far)
        def _():
            for b in range(g * half_blocks, (g + 1) * half_blocks):
                l_copy(b).wait_recv()
                o_copy(b).wait_recv()

        far_cols = jnp.concatenate(
            [far_lse[g * half_blocks + b].T for b in range(half_blocks)], axis=0
        )
        done = []
        for n in range(heads):
            scores = score(qbuf, lo, hi, last_at, keys_end, kmark, last_at, n)
            before = peak_buf[lo:hi, head_cols(n)]
            far_peak = wide(far_cols[:, n : n + 1], before.shape)
            peak = jnp.maximum(jnp.max(scores, axis=-1, keepdims=True), before)
            peak = jnp.maximum(peak, far_peak)
            keep = jnp.exp(before - peak)
            far_weight = jnp.exp(far_peak - peak)
            spread = jnp.concatenate([peak] * (scores.shape[1] // HEAD_DIM), axis=1)
            rows_out, total = mix(jnp.exp(scores - spread), last_at, keys_end, n)
            total = total + total_buf[lo:hi, head_cols(n)] * keep + far_weight
            rows_out = (
                rows_out
                + mixed_buf[lo:hi, head_cols(n)] * keep
                + far_out[lo:hi, head_cols(n)].astype(F32) * far_weight
            )
            done.append((rows_out / total).astype(BF16))
        return jnp.concatenate(done, axis=1)

    def send_parts(g, attended):
        for b in range(half_blocks):
            outgoing[g * half_blocks + b] = jnp.dot(
                attended[b * TILE : (b + 1) * TILE, :],
                wo_theirs[...],
                preferred_element_type=F32,
            ).astype(BF16)
            out_copy(g * half_blocks + b).start()

    def keep_parts(g, attended):
        lo, hi = g * half_rows, (g + 1) * half_rows
        kept[lo:hi, :] = resid[lo:hi, :].astype(F32) + jnp.dot(
            attended, wo_mine[...], preferred_element_type=F32
        )

    first = attend(0)
    send_parts(0, first)
    keep_parts(0, first)
    serve(1)
    second = attend(1)
    send_parts(1, second)
    keep_parts(1, second)

    for b in range(blocks):
        at = slice(b * TILE, (b + 1) * TILE)
        out_copy(b).wait_recv()
        out_ref[at, :] = (kept[at, :] + incoming[b].astype(F32)).astype(BF16)

    for b in range(blocks):
        out_copy(b).wait_send()

    @pl.when(gives_near)
    def _():
        for k in range(DIRECT):
            near_copy(k).wait_send()

    @pl.when(has_near)
    def _():
        for k in range(relays):
            x_copy(k).wait_send()
        for p in range(pieces):
            sink_x(p, h).wait_send()

    @pl.when(serves)
    def _():
        for p in range(pieces):
            sink_z(p).wait_send()
        for b in range(blocks):
            o_copy(b).wait_send()
            l_copy(b).wait_send()

    @pl.when(c == 0)
    def _():
        for p in range(pieces):
            sink_y(p).wait_send()

    @pl.when(has_far)
    def _():
        rule_copy().wait_send()
        for b in range(blocks):
            q_copy(b).wait_send()


def shards(
    tokens, query_weight, key_weight, value_weight, out_weight, block_mask, frame_level, modulation
):
    span, width = tokens.shape
    local = query_weight.shape[1]
    share = width // lax.axis_size("head")
    chunks = span // CHUNK
    relays = chunks - DIRECT
    blocks = span // TILE
    pieces = SINK // 2 // PIECE
    keys = SINK + 2 * span
    dma = pltpu.SemaphoreType.DMA
    anywhere = pl.BlockSpec(memory_space=pl.ANY)
    smem = pl.BlockSpec(memory_space=pltpu.SMEM)
    vmem = pl.BlockSpec(memory_space=pltpu.VMEM)
    return pl.pallas_call(
        functools.partial(layer_kernel, lax.axis_size("frame")),
        out_shape=jax.ShapeDtypeStruct((span, share), BF16),
        in_specs=[anywhere] * 5 + [smem, smem, vmem],
        out_specs=vmem,
        scratch_shapes=[
            pltpu.VMEM((span, width), BF16),
            pltpu.VMEM((span, share), BF16),
            pltpu.VMEM((width, local), BF16),
            pltpu.VMEM((width, local), BF16),
            pltpu.VMEM((width, local), BF16),
            pltpu.VMEM((local, share), BF16),
            pltpu.VMEM((local, share), BF16),
            pltpu.VMEM((span, width), BF16),
            pltpu.VMEM((span, width), BF16),
            pltpu.VMEM((SINK, width), BF16),
            pltpu.VMEM((span, local), BF16),
            pltpu.VMEM((keys, local), BF16),
            pltpu.VMEM((keys, local), BF16),
            pltpu.VMEM((span, TILE), BF16),
            pltpu.VMEM((keys, TILE), BF16),
            pltpu.VMEM((span, TILE), BF16),
            pltpu.VMEM((blocks * 16, TILE), BF16),
            pltpu.VMEM((blocks * 16, TILE), BF16),
            pltpu.VMEM((span, TILE), BF16),
            pltpu.VMEM((span, local), BF16),
            pltpu.VMEM((span, local), BF16),
            pltpu.VMEM((blocks, TILE, TILE), F32),
            pltpu.VMEM((span, local), BF16),
            pltpu.VMEM((blocks, TILE, TILE), F32),
            pltpu.VMEM((span, local), F32),
            pltpu.VMEM((span, local), F32),
            pltpu.VMEM((span, local), F32),
            pltpu.VMEM((blocks, TILE, share), BF16),
            pltpu.VMEM((blocks, TILE, share), BF16),
            pltpu.VMEM((span, share), F32),
            dma((7,)),
            dma((DIRECT,)),
            dma((relays,)),
            dma((chunks,)),
            dma((3 * pieces,)),
            dma((2 * pieces,)),
            dma((blocks,)),
            dma((blocks,)),
            dma((1,)),
            dma((1,)),
            dma((blocks,)),
            dma((blocks,)),
            dma((blocks,)),
            dma((blocks,)),
            dma((blocks,)),
            dma((blocks,)),
        ],
        compiler_params=pltpu.CompilerParams(
            collective_id=0, has_side_effects=True, vmem_limit_bytes=60 * 1024 * 1024
        ),
        name="layer",
    )(
        tokens,
        query_weight,
        key_weight,
        value_weight,
        out_weight,
        block_mask[0],
        frame_level,
        modulation,
    )


def solution(mesh):
    placed = (
        P(("batch", "frame"), None),
        P(None, "head"),
        P(None, "head"),
        P(None, "head"),
        P("head", None),
        P(("batch", "frame"), None, None),
        P(("batch", "frame")),
        P(),
    )
    return jax.shard_map(
        shards, mesh=mesh, in_specs=placed, out_specs=P(("batch", "frame"), "head"), check_vma=False
    )
```

```python
import functools
import math

import jax
import jax.numpy as jnp
from jax import lax
from jax.experimental import pallas as pl
from jax.experimental.pallas import tpu as pltpu
from jax.sharding import PartitionSpec as P

HEAD_DIM = 128
FRAME_TOK = 128
SINK = 128
TILE = 128
CHUNK = 32
DIRECT = 9
EARLY = 4
AHEAD = 4
BATCH = 2 * CHUNK
PIECES = 2
BLOCKED = -1e30
MESH = pl.DeviceIdType.MESH
BF16, F32 = jnp.bfloat16, jnp.float32


def layer_kernel(
    frames,
    tok_hbm,
    wq_hbm,
    wk_hbm,
    wv_hbm,
    wo_hbm,
    mask_ref,
    level_ref,
    table_ref,
    out_ref,
    tok,
    resid,
    wq,
    wk,
    wv,
    wo_mine,
    wo_theirs,
    own,
    near,
    sink,
    qbuf,
    kbuf,
    vbuf,
    qmark,
    kmark,
    ones,
    far_rule,
    their_rule,
    their_mark,
    their_q,
    their_out,
    their_lse,
    far_out,
    far_lse,
    peak_buf,
    total_buf,
    mixed_buf,
    outgoing,
    incoming,
    kept,
    load_sem,
    send_near,
    send_x,
    recv_near,
    send_sink,
    recv_sink,
    send_q,
    recv_q,
    send_rule,
    recv_rule,
    send_o,
    recv_o,
    send_l,
    recv_l,
    send_out,
    recv_out,
):
    c = lax.axis_index("frame")
    h = lax.axis_index("head")
    span, width = own.shape
    local = wq.shape[1]
    share = out_ref.shape[1]
    heads = local // HEAD_DIM
    blocks = span // TILE
    chunks = span // CHUNK
    relays = chunks - DIRECT
    half_rows = span // 2
    half_blocks = blocks // 2
    sink_at, first_at, last_at = span, span + SINK, span + SINK + half_rows
    keys_end = kbuf.shape[0]

    has_near, gives_near = c >= 1, c + 1 < frames
    has_far, serves = c >= 2, c + 2 < frames
    odd, even = c % 2 == 1, c % 2 == 0

    def load(src, dst, i):
        return pltpu.make_async_copy(src, dst, load_sem.at[i])

    my_cols = pl.ds(pl.multiple_of(h * share, share), share)
    their_cols = pl.ds(pl.multiple_of((1 - h) * share, share), share)
    loads = [
        load(tok_hbm, tok, 0),
        load(wq_hbm, wq, 1),
        load(wk_hbm, wk, 2),
        load(wv_hbm, wv, 3),
        load(wo_hbm.at[:, their_cols], wo_theirs, 4),
        load(wo_hbm.at[:, my_cols], wo_mine, 5),
        load(tok_hbm.at[:, my_cols], resid, 6),
    ]
    for one in loads:
        one.start()

    barrier = pltpu.get_barrier_semaphore()
    pl.semaphore_signal(barrier, inc=1, device_id={"head": 1 - h}, device_id_type=MESH)
    expected = 1
    for step in (1, 2):
        for there, valid in ((c - step, c >= step), (c + step, c + step < frames)):

            @pl.when(valid)
            def _():
                pl.semaphore_signal(
                    barrier, inc=1, device_id={"frame": there}, device_id_type=MESH
                )

            expected = expected + jnp.where(valid, 1, 0)

    def rule_rows(j, valid, count):
        lane = lax.broadcasted_iota(jnp.int32, (count, TILE), 1)
        row = jnp.zeros((count, TILE), F32)
        for i in range(blocks):
            seen = mask_ref[i, j]
            if valid is not None:
                seen = seen * jnp.where(valid, 1, 0)
            row = jnp.where(lane == i, jnp.where(seen > 0, 0.0, BLOCKED), row)
        return row.astype(BF16)

    lane_at = lax.broadcasted_iota(jnp.int32, (TILE, TILE), 1)
    for i in range(blocks):
        qmark[i * TILE : (i + 1) * TILE, :] = jnp.where(lane_at == i, 1.0, 0.0).astype(BF16)
    near_tile, own_tile = (SINK + span) // TILE, (SINK + 2 * span) // TILE
    split = TILE + BATCH
    segments = [(own_tile + j, TILE, None) for j in range(blocks)] + [(0, TILE, None)]
    segments += [(near_tile, TILE, has_near), (near_tile + 1, BATCH, has_near)]
    segments += [(near_tile + 3, BATCH, has_near), (near_tile + 1, BATCH, has_near)]
    segments += [(near_tile + 2, TILE, has_near), (near_tile + 3, BATCH, has_near)]
    at = 0
    for j, count, valid in segments:
        kmark[at : at + count, :] = rule_rows(j, valid, count)
        at += count
    for j in range(blocks):
        far_rule[j * 16 : (j + 1) * 16, :] = rule_rows(SINK // TILE + j, None, 16)
    ones[...] = jnp.ones(ones.shape, BF16)

    pl.semaphore_wait(barrier, expected)

    def remote(src, dst, send, recv, device):
        return pltpu.make_async_remote_copy(
            src_ref=src,
            dst_ref=dst,
            send_sem=send,
            recv_sem=recv,
            device_id=device,
            device_id_type=MESH,
        )

    def place_of(half, k):
        if isinstance(k, int):
            low, high = (k, k + 2) if k < 2 else (k + 2, chunks + 1 - k)
            return jnp.where(half == 0, low, high)
        return jnp.where(
            half == 0, jnp.where(k < 2, k, k + 2), jnp.where(k < 2, k + 2, chunks + 1 - k)
        )

    def place(k):
        return place_of(h, k)

    def other_place(k):
        return place_of(1 - h, k)

    def chunk_rows(i):
        return pl.ds(pl.multiple_of(i * CHUNK, CHUNK), CHUNK)

    def near_copy(k):
        at = chunk_rows(place(k))
        return remote(
            own.at[at], near.at[at], send_near.at[k], recv_near.at[place(k)], {"frame": c + 1}
        )

    def x_copy(k):
        at = chunk_rows(place(k))
        return remote(
            near.at[at], near.at[at], send_x.at[k], recv_near.at[place(k)], {"head": 1 - h}
        )

    def x_arrival(k):
        at = chunk_rows(other_place(k))
        return remote(
            near.at[at], near.at[at], send_x.at[k], recv_near.at[other_place(k)], {"head": 1 - h}
        )

    def sink_z(p):
        at = chunk_rows(place(p))
        return remote(
            sink.at[at], sink.at[at], send_sink.at[p], recv_sink.at[place(p)], {"frame": c + 2}
        )

    def sink_y(p):
        at = chunk_rows(place(p))
        return remote(
            sink.at[at],
            sink.at[at],
            send_sink.at[2 * PIECES + p],
            recv_sink.at[place(p)],
            {"frame": c + 1},
        )

    def sink_x(p, half):
        at = chunk_rows(place_of(half, p))
        return remote(
            sink.at[at],
            sink.at[at],
            send_sink.at[PIECES + p],
            recv_sink.at[place_of(half, p)],
            {"head": 1 - h},
        )

    def block_rows(b):
        return pl.ds(pl.multiple_of(b * TILE, TILE), TILE)

    def q_copy(b):
        at = block_rows(b)
        return remote(qbuf.at[at], their_q.at[at], send_q.at[b], recv_q.at[b], {"frame": c - 2})

    def rule_copy():
        return remote(far_rule, their_rule, send_rule.at[0], recv_rule.at[0], {"frame": c - 2})

    def o_copy(b):
        at = block_rows(b)
        return remote(their_out.at[at], far_out.at[at], send_o.at[b], recv_o.at[b], {"frame": c + 2})

    def l_copy(b):
        return remote(
            their_lse.at[b, pl.ds(0, 8)],
            far_lse.at[b, pl.ds(0, 8)],
            send_l.at[b],
            recv_l.at[b],
            {"frame": c + 2},
        )

    def out_copy(b):
        return remote(outgoing.at[b], incoming.at[b], send_out.at[b], recv_out.at[b], {"head": 1 - h})

    def modulate(start, count):
        x = tok[pl.ds(start, count), :].astype(F32)
        mean_square = jnp.mean(x * x, axis=-1, keepdims=True)
        normed = x * lax.rsqrt(mean_square + 1e-06)
        scale_shift = table_ref[level_ref[start // FRAME_TOK]]
        return (normed * (1.0 + scale_shift[0:1]) + scale_shift[1:2]).astype(BF16)

    def batch_at(m):
        middle = (m >= 1) & (m <= chunks // 2 - 2)
        low = jnp.where(m == 0, 0, jnp.where(middle, m + 1, 1))
        high = jnp.where(m == 0, 1, jnp.where(middle, chunks // 2 - m, 0))
        return pl.multiple_of(jnp.where(h == 0, low, high) * BATCH, BATCH)

    def send_near_chunk(k, when):
        if k < DIRECT:

            @pl.when(gives_near & when)
            def _():
                near_copy(k).start()

    loads[0].wait()
    for m in range(AHEAD // 2):
        start = batch_at(m)
        own[pl.ds(start, BATCH), :] = modulate(start, BATCH)
        if m == 0:

            @pl.when(c == 0)
            def _():
                sink[pl.ds(start, BATCH), :] = own[pl.ds(start, BATCH), :]

            @pl.when((c == 0) & serves)
            def _():
                for p in range(PIECES):
                    sink_z(p).start()

        send_near_chunk(2 * m, c >= 0)
        send_near_chunk(2 * m + 1, c >= 0)

    def rest(m, carry):
        start = batch_at(m)
        own[pl.ds(start, BATCH), :] = modulate(start, BATCH)
        return carry

    lax.fori_loop(AHEAD // 2, chunks // 2, rest, 0)
    for k in range(AHEAD, DIRECT):
        send_near_chunk(k, odd)

    def project(flat, weight, dst, start, scale=None):
        res = jnp.dot(flat, weight[...], preferred_element_type=F32)
        if scale is not None:
            res = res * scale
        dst[start : start + flat.shape[0], :] = res.astype(BF16)

    def near_point(k):
        @pl.when(has_near)
        def _():
            near_copy(k).wait_recv()
            if k < relays:
                x_copy(k).start()

        send_near_chunk(k + AHEAD, even)

    def sink_even(p, lo, hi):
        @pl.when(even & (c >= 2 * lo) & (c < 2 * hi))
        def _():
            sink_z(p).wait_recv()

            @pl.when(serves)
            def _():
                sink_z(p).start()

            sink_y(p).start()
            sink_x(p, h).start()

    def sink_odd(p, lo, hi):
        @pl.when(odd & (c >= 2 * lo) & (c < 2 * hi))
        def _():
            sink_y(p).wait_recv()
            sink_x(p, h).start()

    def head_cols(n):
        return slice(n * HEAD_DIM, (n + 1) * HEAD_DIM)

    def score(q_ref, q_at, q_stop, k_at, k_stop, mark, mark_at, n):
        left = jnp.concatenate([q_ref[q_at:q_stop, head_cols(n)], qmark[q_at:q_stop, :]], axis=1)
        marks = mark[mark_at : mark_at + k_stop - k_at, :]
        right = jnp.concatenate([kbuf[k_at:k_stop, head_cols(n)], marks], axis=1)
        return lax.dot_general(left, right, (((1,), (1,)), ((), ())), preferred_element_type=F32)

    def mix(num, k_at, k_stop, n):
        right = jnp.concatenate(
            [vbuf[k_at:k_stop, head_cols(n)], ones[0 : k_stop - k_at, :]], axis=1
        )
        both = jnp.dot(num.astype(BF16), right, preferred_element_type=F32)
        return both[:, :HEAD_DIM], both[:, HEAD_DIM:]

    def wide(column, shape):
        return jnp.broadcast_to(column, shape)

    loads[1].wait()
    project(own[...], wq, qbuf, 0, 1.0 / math.sqrt(HEAD_DIM))

    @pl.when(has_far)
    def _():
        rule_copy().start()
        for b in range(blocks):
            q_copy(b).start()

    near_point(0)
    sink_even(0, 1, 2)
    loads[2].wait()
    project(own[...], wk, kbuf, 0)
    loads[3].wait()
    project(own[...], wv, vbuf, 0)

    def own_heads(lo, hi):
        for n in range(lo, hi):
            scores = score(qbuf, 0, span, 0, span, kmark, 0, n)
            peak = jnp.max(scores, axis=-1, keepdims=True)
            rows_out, total = mix(jnp.exp(scores - peak), 0, span, n)
            peak_buf[:, head_cols(n)] = wide(peak, total.shape)
            total_buf[:, head_cols(n)] = total
            mixed_buf[:, head_cols(n)] = rows_out

    sink_even(1, 1, 2)
    own_heads(0, heads // 2)
    near_point(1)
    sink_even(0, 2, 3)
    own_heads(heads // 2, heads)
    near_point(2)
    sink_even(1, 2, 3)
    sink_odd(0, 1, 2)
    near_point(3)
    sink_even(0, 3, frames)
    sink_odd(1, 1, 2)

    def serve(g):
        lo, hi = g * half_rows, (g + 1) * half_rows

        @pl.when(serves)
        def _():
            if g == 0:
                rule_copy().wait_recv()
                for j in range(blocks):
                    small = their_rule[j * 16 : (j + 1) * 16, :]
                    their_mark[j * TILE : (j + 1) * TILE, :] = jnp.concatenate(
                        [small] * (TILE // 16), axis=0
                    )
            for b in range(g * half_blocks, (g + 1) * half_blocks):
                q_copy(b).wait_recv()
            lanes = lax.broadcasted_iota(jnp.int32, (half_rows, HEAD_DIM), 1)
            lse_all = jnp.zeros((half_rows, HEAD_DIM), F32)
            for n in range(heads):
                scores = score(their_q, lo, hi, 0, span, their_mark, 0, n)
                peak = jnp.max(scores, axis=-1, keepdims=True)
                rows_out, total = mix(jnp.exp(scores - peak), 0, span, n)
                their_out[lo:hi, head_cols(n)] = (rows_out / total).astype(BF16)
                lse_all = jnp.where(lanes == n, peak + jnp.log(total), lse_all)
            for b in range(half_blocks):
                their_lse[g * half_blocks + b] = lse_all[b * TILE : (b + 1) * TILE, :].T
            for b in range(g * half_blocks, (g + 1) * half_blocks):
                l_copy(b).start()
                o_copy(b).start()

    near_point(4)
    sink_even(1, 3, frames)
    sink_odd(0, 2, 3)

    @pl.when(has_near)
    def _():
        for k in range(EARLY):
            x_arrival(k).wait_recv()
        flat = jnp.concatenate([near[0:split, :], near[span - BATCH : span, :]], axis=0)
        project(flat, wk, kbuf, first_at)
        project(flat, wv, vbuf, first_at)

    @pl.when(jnp.logical_not(has_near))
    def _():
        kbuf[first_at:keys_end, :] = jnp.zeros((keys_end - first_at, local), BF16)
        vbuf[first_at:keys_end, :] = jnp.zeros((keys_end - first_at, local), BF16)

    near_point(5)
    sink_odd(1, 2, 3)
    near_point(6)
    sink_odd(0, 3, frames)
    serve(0)
    sink_odd(1, 3, frames)

    @pl.when(has_far)
    def _():
        for p in range(PIECES):
            sink_x(p, 1 - h).wait_recv()

    @pl.when(c == 0)
    def _():
        at = pl.ds(pl.multiple_of((1 - h) * BATCH, BATCH), BATCH)
        sink[at, :] = own[at, :]

    @pl.when(c == 1)
    def _():
        sink[...] = near[0:SINK, :]

    project(sink[...], wk, kbuf, sink_at)
    project(sink[...], wv, vbuf, sink_at)

    for n in range(heads):
        scores = score(qbuf, 0, span, sink_at, last_at, kmark, sink_at, n)
        before = peak_buf[:, head_cols(n)]
        peak = jnp.maximum(jnp.max(scores, axis=-1, keepdims=True), before)
        keep = jnp.exp(before - peak)
        spread = jnp.concatenate([peak] * (scores.shape[1] // HEAD_DIM), axis=1)
        rows_out, total = mix(jnp.exp(scores - spread), sink_at, last_at, n)
        peak_buf[:, head_cols(n)] = peak
        total_buf[:, head_cols(n)] = total_buf[:, head_cols(n)] * keep + total
        mixed_buf[:, head_cols(n)] = mixed_buf[:, head_cols(n)] * keep + rows_out

    for i in (4, 5, 6):
        loads[i].wait()

    @pl.when(has_near)
    def _():
        for k in range(relays, DIRECT):
            near_copy(k).wait_recv()
        for k in range(EARLY, relays):
            x_arrival(k).wait_recv()
        flat = near[split : span - BATCH, :]
        project(flat, wk, kbuf, last_at)
        project(flat, wv, vbuf, last_at)

    @pl.when(jnp.logical_not(has_far))
    def _():
        far_out[...] = jnp.zeros(far_out.shape, BF16)
        far_lse[...] = jnp.full(far_lse.shape, BLOCKED, F32)

    def attend(g):
        lo, hi = g * half_rows, (g + 1) * half_rows

        @pl.when(has_far)
        def _():
            for b in range(g * half_blocks, (g + 1) * half_blocks):
                l_copy(b).wait_recv()
                o_copy(b).wait_recv()

        far_cols = jnp.concatenate(
            [far_lse[g * half_blocks + b].T for b in range(half_blocks)], axis=0
        )
        done = []
        for n in range(heads):
            scores = score(qbuf, lo, hi, last_at, keys_end, kmark, last_at, n)
            before = peak_buf[lo:hi, head_cols(n)]
            far_peak = wide(far_cols[:, n : n + 1], before.shape)
            peak = jnp.maximum(jnp.max(scores, axis=-1, keepdims=True), before)
            peak = jnp.maximum(peak, far_peak)
            keep = jnp.exp(before - peak)
            far_weight = jnp.exp(far_peak - peak)
            spread = jnp.concatenate([peak] * (scores.shape[1] // HEAD_DIM), axis=1)
            rows_out, total = mix(jnp.exp(scores - spread), last_at, keys_end, n)
            total = total + total_buf[lo:hi, head_cols(n)] * keep + far_weight
            rows_out = (
                rows_out
                + mixed_buf[lo:hi, head_cols(n)] * keep
                + far_out[lo:hi, head_cols(n)].astype(F32) * far_weight
            )
            done.append((rows_out / total).astype(BF16))
        return jnp.concatenate(done, axis=1)

    def send_parts(g, attended):
        for b in range(half_blocks):
            outgoing[g * half_blocks + b] = jnp.dot(
                attended[b * TILE : (b + 1) * TILE, :],
                wo_theirs[...],
                preferred_element_type=F32,
            ).astype(BF16)
            out_copy(g * half_blocks + b).start()

    def keep_parts(g, attended):
        lo, hi = g * half_rows, (g + 1) * half_rows
        kept[lo:hi, :] = resid[lo:hi, :].astype(F32) + jnp.dot(
            attended, wo_mine[...], preferred_element_type=F32
        )

    first = attend(0)
    send_parts(0, first)
    keep_parts(0, first)
    serve(1)
    second = attend(1)
    send_parts(1, second)
    keep_parts(1, second)

    for b in range(blocks):
        at = slice(b * TILE, (b + 1) * TILE)
        out_copy(b).wait_recv()
        out_ref[at, :] = (kept[at, :] + incoming[b].astype(F32)).astype(BF16)

    for b in range(blocks):
        out_copy(b).wait_send()

    @pl.when(gives_near)
    def _():
        for k in range(DIRECT):
            near_copy(k).wait_send()

    @pl.when(has_near)
    def _():
        for k in range(relays):
            x_copy(k).wait_send()

    @pl.when(serves & even)
    def _():
        for p in range(PIECES):
            sink_z(p).wait_send()

    @pl.when(serves)
    def _():
        for b in range(blocks):
            o_copy(b).wait_send()
            l_copy(b).wait_send()

    @pl.when(has_far)
    def _():
        for p in range(PIECES):
            sink_x(p, h).wait_send()

    @pl.when(has_far & even)
    def _():
        for p in range(PIECES):
            sink_y(p).wait_send()

    @pl.when(has_far)
    def _():
        rule_copy().wait_send()
        for b in range(blocks):
            q_copy(b).wait_send()


def shards(
    tokens, query_weight, key_weight, value_weight, out_weight, block_mask, frame_level, modulation
):
    span, width = tokens.shape
    local = query_weight.shape[1]
    share = width // lax.axis_size("head")
    chunks = span // CHUNK
    relays = chunks - DIRECT
    blocks = span // TILE
    keys = SINK + 2 * span
    dma = pltpu.SemaphoreType.DMA
    anywhere = pl.BlockSpec(memory_space=pl.ANY)
    smem = pl.BlockSpec(memory_space=pltpu.SMEM)
    vmem = pl.BlockSpec(memory_space=pltpu.VMEM)
    return pl.pallas_call(
        functools.partial(layer_kernel, lax.axis_size("frame")),
        out_shape=jax.ShapeDtypeStruct((span, share), BF16),
        in_specs=[anywhere] * 5 + [smem, smem, vmem],
        out_specs=vmem,
        scratch_shapes=[
            pltpu.VMEM((span, width), BF16),
            pltpu.VMEM((span, share), BF16),
            pltpu.VMEM((width, local), BF16),
            pltpu.VMEM((width, local), BF16),
            pltpu.VMEM((width, local), BF16),
            pltpu.VMEM((local, share), BF16),
            pltpu.VMEM((local, share), BF16),
            pltpu.VMEM((span, width), BF16),
            pltpu.VMEM((span, width), BF16),
            pltpu.VMEM((SINK, width), BF16),
            pltpu.VMEM((span, local), BF16),
            pltpu.VMEM((keys, local), BF16),
            pltpu.VMEM((keys, local), BF16),
            pltpu.VMEM((span, TILE), BF16),
            pltpu.VMEM((keys, TILE), BF16),
            pltpu.VMEM((span, TILE), BF16),
            pltpu.VMEM((blocks * 16, TILE), BF16),
            pltpu.VMEM((blocks * 16, TILE), BF16),
            pltpu.VMEM((span, TILE), BF16),
            pltpu.VMEM((span, local), BF16),
            pltpu.VMEM((span, local), BF16),
            pltpu.VMEM((blocks, TILE, TILE), F32),
            pltpu.VMEM((span, local), BF16),
            pltpu.VMEM((blocks, TILE, TILE), F32),
            pltpu.VMEM((span, local), F32),
            pltpu.VMEM((span, local), F32),
            pltpu.VMEM((span, local), F32),
            pltpu.VMEM((blocks, TILE, share), BF16),
            pltpu.VMEM((blocks, TILE, share), BF16),
            pltpu.VMEM((span, share), F32),
            dma((7,)),
            dma((DIRECT,)),
            dma((relays,)),
            dma((chunks,)),
            dma((3 * PIECES,)),
            dma((2 * PIECES,)),
            dma((blocks,)),
            dma((blocks,)),
            dma((1,)),
            dma((1,)),
            dma((blocks,)),
            dma((blocks,)),
            dma((blocks,)),
            dma((blocks,)),
            dma((blocks,)),
            dma((blocks,)),
        ],
        compiler_params=pltpu.CompilerParams(
            collective_id=0, has_side_effects=True, vmem_limit_bytes=60 * 1024 * 1024
        ),
        name="layer",
    )(
        tokens,
        query_weight,
        key_weight,
        value_weight,
        out_weight,
        block_mask[0],
        frame_level,
        modulation,
    )


def solution(mesh):
    placed = (
        P(("batch", "frame"), None),
        P(None, "head"),
        P(None, "head"),
        P(None, "head"),
        P("head", None),
        P(("batch", "frame"), None, None),
        P(("batch", "frame")),
        P(),
    )
    return jax.shard_map(
        shards, mesh=mesh, in_specs=placed, out_specs=P(("batch", "frame"), "head"), check_vma=False
    )
```

```python
import functools
import math

import jax
import jax.numpy as jnp
from jax import lax
from jax.experimental import pallas as pl
from jax.experimental.pallas import tpu as pltpu
from jax.sharding import PartitionSpec as P

HEAD_DIM = 128
FRAME_TOK = 128
SINK = 128
TILE = 128
CHUNK = 32
DIRECT = 9
EARLY = 4
AHEAD = 2
BATCH = 2 * CHUNK
PIECES = 2
BLOCKED = -1e30
MESH = pl.DeviceIdType.MESH
BF16, F32 = jnp.bfloat16, jnp.float32


def layer_kernel(
    frames,
    tok_hbm,
    wq_hbm,
    wk_hbm,
    wv_hbm,
    wo_hbm,
    mask_ref,
    level_ref,
    table_ref,
    out_ref,
    tok,
    resid,
    wq,
    wk,
    wv,
    wo_mine,
    wo_theirs,
    own,
    near,
    sink,
    qbuf,
    kbuf,
    vbuf,
    qmark,
    kmark,
    ones,
    far_rule,
    their_rule,
    their_mark,
    their_q,
    their_out,
    their_lse,
    far_out,
    far_lse,
    peak_buf,
    total_buf,
    mixed_buf,
    outgoing,
    incoming,
    kept,
    load_sem,
    send_near,
    send_x,
    recv_near,
    send_sink,
    recv_sink,
    send_q,
    recv_q,
    send_rule,
    recv_rule,
    send_o,
    recv_o,
    send_l,
    recv_l,
    send_out,
    recv_out,
):
    c = lax.axis_index("frame")
    h = lax.axis_index("head")
    span, width = own.shape
    local = wq.shape[1]
    share = out_ref.shape[1]
    heads = local // HEAD_DIM
    blocks = span // TILE
    chunks = span // CHUNK
    relays = chunks - DIRECT
    half_rows = span // 2
    half_blocks = blocks // 2
    sink_at, first_at, last_at = span, span + SINK, span + SINK + half_rows
    keys_end = kbuf.shape[0]

    has_near, gives_near = c >= 1, c + 1 < frames
    has_far, serves = c >= 2, c + 2 < frames
    odd, even = c % 2 == 1, c % 2 == 0

    def load(src, dst, i):
        return pltpu.make_async_copy(src, dst, load_sem.at[i])

    my_cols = pl.ds(pl.multiple_of(h * share, share), share)
    their_cols = pl.ds(pl.multiple_of((1 - h) * share, share), share)
    loads = [
        load(tok_hbm, tok, 0),
        load(wq_hbm, wq, 1),
        load(wk_hbm, wk, 2),
        load(wv_hbm, wv, 3),
        load(wo_hbm.at[:, their_cols], wo_theirs, 4),
        load(wo_hbm.at[:, my_cols], wo_mine, 5),
        load(tok_hbm.at[:, my_cols], resid, 6),
    ]
    for one in loads:
        one.start()

    barrier = pltpu.get_barrier_semaphore()
    pl.semaphore_signal(barrier, inc=1, device_id={"head": 1 - h}, device_id_type=MESH)
    expected = 1
    for step in (1, 2):
        for there, valid in ((c - step, c >= step), (c + step, c + step < frames)):

            @pl.when(valid)
            def _():
                pl.semaphore_signal(
                    barrier, inc=1, device_id={"frame": there}, device_id_type=MESH
                )

            expected = expected + jnp.where(valid, 1, 0)

    def rule_rows(j, valid, count):
        lane = lax.broadcasted_iota(jnp.int32, (count, TILE), 1)
        row = jnp.zeros((count, TILE), F32)
        for i in range(blocks):
            seen = mask_ref[i, j]
            if valid is not None:
                seen = seen * jnp.where(valid, 1, 0)
            row = jnp.where(lane == i, jnp.where(seen > 0, 0.0, BLOCKED), row)
        return row.astype(BF16)

    lane_at = lax.broadcasted_iota(jnp.int32, (TILE, TILE), 1)
    for i in range(blocks):
        qmark[i * TILE : (i + 1) * TILE, :] = jnp.where(lane_at == i, 1.0, 0.0).astype(BF16)
    near_tile, own_tile = (SINK + span) // TILE, (SINK + 2 * span) // TILE
    split = TILE + BATCH
    segments = [(own_tile + j, TILE, None) for j in range(blocks)] + [(0, TILE, None)]
    segments += [(near_tile, TILE, has_near), (near_tile + 1, BATCH, has_near)]
    segments += [(near_tile + 3, BATCH, has_near), (near_tile + 1, BATCH, has_near)]
    segments += [(near_tile + 2, TILE, has_near), (near_tile + 3, BATCH, has_near)]
    at = 0
    for j, count, valid in segments:
        kmark[at : at + count, :] = rule_rows(j, valid, count)
        at += count
    for j in range(blocks):
        far_rule[j * 16 : (j + 1) * 16, :] = rule_rows(SINK // TILE + j, None, 16)
    ones[...] = jnp.ones(ones.shape, BF16)

    pl.semaphore_wait(barrier, expected)

    def remote(src, dst, send, recv, device):
        return pltpu.make_async_remote_copy(
            src_ref=src,
            dst_ref=dst,
            send_sem=send,
            recv_sem=recv,
            device_id=device,
            device_id_type=MESH,
        )

    def place_of(half, k):
        if isinstance(k, int):
            low, high = (k, k + 2) if k < 2 else (k + 2, chunks + 1 - k)
            return jnp.where(half == 0, low, high)
        return jnp.where(
            half == 0, jnp.where(k < 2, k, k + 2), jnp.where(k < 2, k + 2, chunks + 1 - k)
        )

    def place(k):
        return place_of(h, k)

    def other_place(k):
        return place_of(1 - h, k)

    def chunk_rows(i):
        return pl.ds(pl.multiple_of(i * CHUNK, CHUNK), CHUNK)

    def near_copy(k):
        at = chunk_rows(place(k))
        return remote(
            own.at[at], near.at[at], send_near.at[k], recv_near.at[place(k)], {"frame": c + 1}
        )

    def x_copy(k):
        at = chunk_rows(place(k))
        return remote(
            near.at[at], near.at[at], send_x.at[k], recv_near.at[place(k)], {"head": 1 - h}
        )

    def x_arrival(k):
        at = chunk_rows(other_place(k))
        return remote(
            near.at[at], near.at[at], send_x.at[k], recv_near.at[other_place(k)], {"head": 1 - h}
        )

    def sink_z(p):
        at = chunk_rows(place(p))
        return remote(
            sink.at[at], sink.at[at], send_sink.at[p], recv_sink.at[place(p)], {"frame": c + 2}
        )

    def sink_y(p):
        at = chunk_rows(place(p))
        return remote(
            sink.at[at],
            sink.at[at],
            send_sink.at[2 * PIECES + p],
            recv_sink.at[place(p)],
            {"frame": c + 1},
        )

    def sink_x(p, half):
        at = chunk_rows(place_of(half, p))
        return remote(
            sink.at[at],
            sink.at[at],
            send_sink.at[PIECES + p],
            recv_sink.at[place_of(half, p)],
            {"head": 1 - h},
        )

    def block_rows(b):
        return pl.ds(pl.multiple_of(b * TILE, TILE), TILE)

    def q_copy(b):
        at = block_rows(b)
        return remote(qbuf.at[at], their_q.at[at], send_q.at[b], recv_q.at[b], {"frame": c - 2})

    def rule_copy():
        return remote(far_rule, their_rule, send_rule.at[0], recv_rule.at[0], {"frame": c - 2})

    def o_copy(b):
        at = block_rows(b)
        return remote(their_out.at[at], far_out.at[at], send_o.at[b], recv_o.at[b], {"frame": c + 2})

    def l_copy(b):
        return remote(
            their_lse.at[b, pl.ds(0, 8)],
            far_lse.at[b, pl.ds(0, 8)],
            send_l.at[b],
            recv_l.at[b],
            {"frame": c + 2},
        )

    def out_copy(b):
        return remote(outgoing.at[b], incoming.at[b], send_out.at[b], recv_out.at[b], {"head": 1 - h})

    def modulate(start, count):
        x = tok[pl.ds(start, count), :].astype(F32)
        mean_square = jnp.mean(x * x, axis=-1, keepdims=True)
        normed = x * lax.rsqrt(mean_square + 1e-06)
        scale_shift = table_ref[level_ref[start // FRAME_TOK]]
        return (normed * (1.0 + scale_shift[0:1]) + scale_shift[1:2]).astype(BF16)

    def batch_at(m):
        middle = (m >= 1) & (m <= chunks // 2 - 2)
        low = jnp.where(m == 0, 0, jnp.where(middle, m + 1, 1))
        high = jnp.where(m == 0, 1, jnp.where(middle, chunks // 2 - m, 0))
        return pl.multiple_of(jnp.where(h == 0, low, high) * BATCH, BATCH)

    def send_near_chunk(k, when):
        if k < DIRECT:

            @pl.when(gives_near & when)
            def _():
                near_copy(k).start()

    loads[0].wait()
    for m in range(AHEAD // 2):
        start = batch_at(m)
        own[pl.ds(start, BATCH), :] = modulate(start, BATCH)
        if m == 0:

            @pl.when(c == 0)
            def _():
                sink[pl.ds(start, BATCH), :] = own[pl.ds(start, BATCH), :]

            @pl.when((c == 0) & serves)
            def _():
                for p in range(PIECES):
                    sink_z(p).start()

        send_near_chunk(2 * m, c >= 0)
        send_near_chunk(2 * m + 1, c >= 0)

    def rest(m, carry):
        start = batch_at(m)
        own[pl.ds(start, BATCH), :] = modulate(start, BATCH)
        return carry

    lax.fori_loop(AHEAD // 2, chunks // 2, rest, 0)
    for k in range(AHEAD, DIRECT):
        send_near_chunk(k, odd)

    def project(flat, weight, dst, start, scale=None):
        res = jnp.dot(flat, weight[...], preferred_element_type=F32)
        if scale is not None:
            res = res * scale
        dst[start : start + flat.shape[0], :] = res.astype(BF16)

    def near_point(k):
        @pl.when(has_near)
        def _():
            near_copy(k).wait_recv()
            if k < relays:
                x_copy(k).start()

        send_near_chunk(k + AHEAD, even)

    def sink_even(p, lo, hi):
        @pl.when(even & (c >= 2 * lo) & (c < 2 * hi))
        def _():
            sink_z(p).wait_recv()

            @pl.when(serves)
            def _():
                sink_z(p).start()

            sink_y(p).start()
            sink_x(p, h).start()

    def sink_odd(p, lo, hi):
        @pl.when(odd & (c >= 2 * lo) & (c < 2 * hi))
        def _():
            sink_y(p).wait_recv()
            sink_x(p, h).start()

    def head_cols(n):
        return slice(n * HEAD_DIM, (n + 1) * HEAD_DIM)

    def score(q_ref, q_at, q_stop, k_at, k_stop, mark, mark_at, n):
        left = jnp.concatenate([q_ref[q_at:q_stop, head_cols(n)], qmark[q_at:q_stop, :]], axis=1)
        marks = mark[mark_at : mark_at + k_stop - k_at, :]
        right = jnp.concatenate([kbuf[k_at:k_stop, head_cols(n)], marks], axis=1)
        return lax.dot_general(left, right, (((1,), (1,)), ((), ())), preferred_element_type=F32)

    def mix(num, k_at, k_stop, n):
        right = jnp.concatenate(
            [vbuf[k_at:k_stop, head_cols(n)], ones[0 : k_stop - k_at, :]], axis=1
        )
        both = jnp.dot(num.astype(BF16), right, preferred_element_type=F32)
        return both[:, :HEAD_DIM], both[:, HEAD_DIM:]

    def wide(column, shape):
        return jnp.broadcast_to(column, shape)

    loads[1].wait()
    project(own[...], wq, qbuf, 0, 1.0 / math.sqrt(HEAD_DIM))

    @pl.when(has_far)
    def _():
        rule_copy().start()
        for b in range(blocks):
            q_copy(b).start()

    near_point(0)
    sink_even(0, 1, 2)
    loads[2].wait()
    project(own[...], wk, kbuf, 0)
    loads[3].wait()
    project(own[...], wv, vbuf, 0)

    def own_heads(lo, hi):
        for n in range(lo, hi):
            scores = score(qbuf, 0, span, 0, span, kmark, 0, n)
            peak = jnp.max(scores, axis=-1, keepdims=True)
            rows_out, total = mix(jnp.exp(scores - peak), 0, span, n)
            peak_buf[:, head_cols(n)] = wide(peak, total.shape)
            total_buf[:, head_cols(n)] = total
            mixed_buf[:, head_cols(n)] = rows_out

    sink_even(1, 1, 2)
    own_heads(0, heads // 2)
    near_point(1)
    sink_even(0, 2, 3)
    own_heads(heads // 2, heads)
    near_point(2)
    sink_even(1, 2, 3)
    sink_odd(0, 1, 2)
    near_point(3)
    sink_even(0, 3, frames)
    sink_odd(1, 1, 2)

    def serve(g):
        lo, hi = g * half_rows, (g + 1) * half_rows

        @pl.when(serves)
        def _():
            if g == 0:
                rule_copy().wait_recv()
                for j in range(blocks):
                    small = their_rule[j * 16 : (j + 1) * 16, :]
                    their_mark[j * TILE : (j + 1) * TILE, :] = jnp.concatenate(
                        [small] * (TILE // 16), axis=0
                    )
            for b in range(g * half_blocks, (g + 1) * half_blocks):
                q_copy(b).wait_recv()
            lanes = lax.broadcasted_iota(jnp.int32, (half_rows, HEAD_DIM), 1)
            lse_all = jnp.zeros((half_rows, HEAD_DIM), F32)
            for n in range(heads):
                scores = score(their_q, lo, hi, 0, span, their_mark, 0, n)
                peak = jnp.max(scores, axis=-1, keepdims=True)
                rows_out, total = mix(jnp.exp(scores - peak), 0, span, n)
                their_out[lo:hi, head_cols(n)] = (rows_out / total).astype(BF16)
                lse_all = jnp.where(lanes == n, peak + jnp.log(total), lse_all)
            for b in range(half_blocks):
                their_lse[g * half_blocks + b] = lse_all[b * TILE : (b + 1) * TILE, :].T
            for b in range(g * half_blocks, (g + 1) * half_blocks):
                l_copy(b).start()
                o_copy(b).start()

    near_point(4)
    sink_even(1, 3, frames)
    sink_odd(0, 2, 3)

    @pl.when(has_near)
    def _():
        for k in range(EARLY):
            x_arrival(k).wait_recv()
        flat = jnp.concatenate([near[0:split, :], near[span - BATCH : span, :]], axis=0)
        project(flat, wk, kbuf, first_at)
        project(flat, wv, vbuf, first_at)

    @pl.when(jnp.logical_not(has_near))
    def _():
        kbuf[first_at:keys_end, :] = jnp.zeros((keys_end - first_at, local), BF16)
        vbuf[first_at:keys_end, :] = jnp.zeros((keys_end - first_at, local), BF16)

    near_point(5)
    sink_odd(1, 2, 3)
    near_point(6)
    sink_odd(0, 3, frames)
    serve(0)
    sink_odd(1, 3, frames)

    @pl.when(has_far)
    def _():
        for p in range(PIECES):
            sink_x(p, 1 - h).wait_recv()

    @pl.when(c == 0)
    def _():
        at = pl.ds(pl.multiple_of((1 - h) * BATCH, BATCH), BATCH)
        sink[at, :] = own[at, :]

    @pl.when(c == 1)
    def _():
        sink[...] = near[0:SINK, :]

    project(sink[...], wk, kbuf, sink_at)
    project(sink[...], wv, vbuf, sink_at)

    for n in range(heads):
        scores = score(qbuf, 0, span, sink_at, last_at, kmark, sink_at, n)
        before = peak_buf[:, head_cols(n)]
        peak = jnp.maximum(jnp.max(scores, axis=-1, keepdims=True), before)
        keep = jnp.exp(before - peak)
        spread = jnp.concatenate([peak] * (scores.shape[1] // HEAD_DIM), axis=1)
        rows_out, total = mix(jnp.exp(scores - spread), sink_at, last_at, n)
        peak_buf[:, head_cols(n)] = peak
        total_buf[:, head_cols(n)] = total_buf[:, head_cols(n)] * keep + total
        mixed_buf[:, head_cols(n)] = mixed_buf[:, head_cols(n)] * keep + rows_out

    for i in (4, 5, 6):
        loads[i].wait()

    @pl.when(has_near)
    def _():
        for k in range(relays, DIRECT):
            near_copy(k).wait_recv()
        for k in range(EARLY, relays):
            x_arrival(k).wait_recv()
        flat = near[split : span - BATCH, :]
        project(flat, wk, kbuf, last_at)
        project(flat, wv, vbuf, last_at)

    @pl.when(jnp.logical_not(has_far))
    def _():
        far_out[...] = jnp.zeros(far_out.shape, BF16)
        far_lse[...] = jnp.full(far_lse.shape, BLOCKED, F32)

    def last_keys(g):
        lo, hi = g * half_rows, (g + 1) * half_rows
        for n in range(heads):
            scores = score(qbuf, lo, hi, last_at, keys_end, kmark, last_at, n)
            before = peak_buf[lo:hi, head_cols(n)]
            peak = jnp.maximum(jnp.max(scores, axis=-1, keepdims=True), before)
            keep = jnp.exp(before - peak)
            spread = jnp.concatenate([peak] * (scores.shape[1] // HEAD_DIM), axis=1)
            rows_out, total = mix(jnp.exp(scores - spread), last_at, keys_end, n)
            peak_buf[lo:hi, head_cols(n)] = peak
            total_buf[lo:hi, head_cols(n)] = total_buf[lo:hi, head_cols(n)] * keep + total
            mixed_buf[lo:hi, head_cols(n)] = mixed_buf[lo:hi, head_cols(n)] * keep + rows_out

    def send_block(b):
        lo, hi = b * TILE, (b + 1) * TILE

        @pl.when(has_far)
        def _():
            l_copy(b).wait_recv()
            o_copy(b).wait_recv()

        far_cols = far_lse[b].T
        done = []
        for n in range(heads):
            before = peak_buf[lo:hi, head_cols(n)]
            far_peak = wide(far_cols[:, n : n + 1], before.shape)
            peak = jnp.maximum(before, far_peak)
            keep = jnp.exp(before - peak)
            far_weight = jnp.exp(far_peak - peak)
            total = total_buf[lo:hi, head_cols(n)] * keep + far_weight
            rows_out = (
                mixed_buf[lo:hi, head_cols(n)] * keep
                + far_out[lo:hi, head_cols(n)].astype(F32) * far_weight
            )
            done.append((rows_out / total).astype(BF16))
        attended = jnp.concatenate(done, axis=1)
        outgoing[b] = jnp.dot(attended, wo_theirs[...], preferred_element_type=F32).astype(BF16)
        out_copy(b).start()
        return attended

    def keep_block(b, attended):
        lo, hi = b * TILE, (b + 1) * TILE
        kept[lo:hi, :] = resid[lo:hi, :].astype(F32) + jnp.dot(
            attended, wo_mine[...], preferred_element_type=F32
        )

    last_keys(0)
    first = send_block(0)
    serve(1)
    second = send_block(1)
    keep_block(0, first)
    last_keys(1)
    keep_block(1, second)
    for b in range(half_blocks, blocks):
        keep_block(b, send_block(b))

    for b in range(blocks):
        at = slice(b * TILE, (b + 1) * TILE)
        out_copy(b).wait_recv()
        out_ref[at, :] = (kept[at, :] + incoming[b].astype(F32)).astype(BF16)

    for b in range(blocks):
        out_copy(b).wait_send()

    @pl.when(gives_near)
    def _():
        for k in range(DIRECT):
            near_copy(k).wait_send()

    @pl.when(has_near)
    def _():
        for k in range(relays):
            x_copy(k).wait_send()

    @pl.when(serves & even)
    def _():
        for p in range(PIECES):
            sink_z(p).wait_send()

    @pl.when(serves)
    def _():
        for b in range(blocks):
            o_copy(b).wait_send()
            l_copy(b).wait_send()

    @pl.when(has_far)
    def _():
        for p in range(PIECES):
            sink_x(p, h).wait_send()

    @pl.when(has_far & even)
    def _():
        for p in range(PIECES):
            sink_y(p).wait_send()

    @pl.when(has_far)
    def _():
        rule_copy().wait_send()
        for b in range(blocks):
            q_copy(b).wait_send()


def shards(
    tokens, query_weight, key_weight, value_weight, out_weight, block_mask, frame_level, modulation
):
    span, width = tokens.shape
    local = query_weight.shape[1]
    share = width // lax.axis_size("head")
    chunks = span // CHUNK
    relays = chunks - DIRECT
    blocks = span // TILE
    keys = SINK + 2 * span
    dma = pltpu.SemaphoreType.DMA
    anywhere = pl.BlockSpec(memory_space=pl.ANY)
    smem = pl.BlockSpec(memory_space=pltpu.SMEM)
    vmem = pl.BlockSpec(memory_space=pltpu.VMEM)
    return pl.pallas_call(
        functools.partial(layer_kernel, lax.axis_size("frame")),
        out_shape=jax.ShapeDtypeStruct((span, share), BF16),
        in_specs=[anywhere] * 5 + [smem, smem, vmem],
        out_specs=vmem,
        scratch_shapes=[
            pltpu.VMEM((span, width), BF16),
            pltpu.VMEM((span, share), BF16),
            pltpu.VMEM((width, local), BF16),
            pltpu.VMEM((width, local), BF16),
            pltpu.VMEM((width, local), BF16),
            pltpu.VMEM((local, share), BF16),
            pltpu.VMEM((local, share), BF16),
            pltpu.VMEM((span, width), BF16),
            pltpu.VMEM((span, width), BF16),
            pltpu.VMEM((SINK, width), BF16),
            pltpu.VMEM((span, local), BF16),
            pltpu.VMEM((keys, local), BF16),
            pltpu.VMEM((keys, local), BF16),
            pltpu.VMEM((span, TILE), BF16),
            pltpu.VMEM((keys, TILE), BF16),
            pltpu.VMEM((span, TILE), BF16),
            pltpu.VMEM((blocks * 16, TILE), BF16),
            pltpu.VMEM((blocks * 16, TILE), BF16),
            pltpu.VMEM((span, TILE), BF16),
            pltpu.VMEM((span, local), BF16),
            pltpu.VMEM((span, local), BF16),
            pltpu.VMEM((blocks, TILE, TILE), F32),
            pltpu.VMEM((span, local), BF16),
            pltpu.VMEM((blocks, TILE, TILE), F32),
            pltpu.VMEM((span, local), F32),
            pltpu.VMEM((span, local), F32),
            pltpu.VMEM((span, local), F32),
            pltpu.VMEM((blocks, TILE, share), BF16),
            pltpu.VMEM((blocks, TILE, share), BF16),
            pltpu.VMEM((span, share), F32),
            dma((7,)),
            dma((DIRECT,)),
            dma((relays,)),
            dma((chunks,)),
            dma((3 * PIECES,)),
            dma((2 * PIECES,)),
            dma((blocks,)),
            dma((blocks,)),
            dma((1,)),
            dma((1,)),
            dma((blocks,)),
            dma((blocks,)),
            dma((blocks,)),
            dma((blocks,)),
            dma((blocks,)),
            dma((blocks,)),
        ],
        compiler_params=pltpu.CompilerParams(
            collective_id=0, has_side_effects=True, vmem_limit_bytes=60 * 1024 * 1024
        ),
        name="layer",
    )(
        tokens,
        query_weight,
        key_weight,
        value_weight,
        out_weight,
        block_mask[0],
        frame_level,
        modulation,
    )


def solution(mesh):
    placed = (
        P(("batch", "frame"), None),
        P(None, "head"),
        P(None, "head"),
        P(None, "head"),
        P("head", None),
        P(("batch", "frame"), None, None),
        P(("batch", "frame")),
        P(),
    )
    return jax.shard_map(
        shards, mesh=mesh, in_specs=placed, out_specs=P(("batch", "frame"), "head"), check_vma=False
    )
```

```python
import functools
import math

import jax
import jax.numpy as jnp
from jax import lax
from jax.experimental import pallas as pl
from jax.experimental.pallas import tpu as pltpu
from jax.sharding import PartitionSpec as P

HEAD_DIM = 128
FRAME_TOK = 128
SINK = 128
TILE = 128
CHUNK = 32
DIRECT = 9
EARLY = 4
AHEAD = 2
BATCH = 2 * CHUNK
PIECES = 2
BLOCKED = -1e30
MESH = pl.DeviceIdType.MESH
BF16, F32 = jnp.bfloat16, jnp.float32


def layer_kernel(
    frames,
    tok_hbm,
    wq_hbm,
    wk_hbm,
    wv_hbm,
    wo_hbm,
    mask_ref,
    level_ref,
    table_hbm,
    out_hbm,
    table_ref,
    done,
    tok,
    resid,
    wq,
    wk,
    wv,
    wo_mine,
    wo_theirs,
    own,
    near,
    sink,
    qbuf,
    kbuf,
    vbuf,
    qmark,
    kmark,
    ones,
    far_rule,
    their_rule,
    their_mark,
    their_q,
    their_out,
    their_lse,
    far_out,
    far_lse,
    peak_buf,
    total_buf,
    mixed_buf,
    outgoing,
    incoming,
    kept,
    load_sem,
    store_sem,
    send_near,
    send_x,
    recv_near,
    send_sink,
    recv_sink,
    send_q,
    recv_q,
    send_rule,
    recv_rule,
    send_o,
    recv_o,
    send_l,
    recv_l,
    send_out,
    recv_out,
):
    c = lax.axis_index("frame")
    h = lax.axis_index("head")
    span, width = own.shape
    local = wq.shape[1]
    share = done.shape[1]
    heads = local // HEAD_DIM
    blocks = span // TILE
    chunks = span // CHUNK
    relays = chunks - DIRECT
    half_rows = span // 2
    half_blocks = blocks // 2
    first_at, sink_at, last_at = span, span + half_rows, span + half_rows + SINK
    keys_end = kbuf.shape[0]

    has_near, gives_near = c >= 1, c + 1 < frames
    has_far, serves = c >= 2, c + 2 < frames
    odd, even = c % 2 == 1, c % 2 == 0

    def load(src, dst, i):
        return pltpu.make_async_copy(src, dst, load_sem.at[i])

    my_cols = pl.ds(pl.multiple_of(h * share, share), share)
    their_cols = pl.ds(pl.multiple_of((1 - h) * share, share), share)
    loads = [
        load(tok_hbm, tok, 0),
        load(wq_hbm, wq, 1),
        load(wk_hbm, wk, 2),
        load(wv_hbm, wv, 3),
        load(wo_hbm.at[:, their_cols], wo_theirs, 4),
        load(wo_hbm.at[:, my_cols], wo_mine, 5),
        load(tok_hbm.at[:, my_cols], resid, 6),
        load(table_hbm, table_ref, 7),
    ]
    for i in (0, 7, 1, 2, 3, 4, 5, 6):
        loads[i].start()

    barrier = pltpu.get_barrier_semaphore()
    pl.semaphore_signal(barrier, inc=1, device_id={"head": 1 - h}, device_id_type=MESH)
    expected = 1
    for step in (1, 2):
        for there, valid in ((c - step, c >= step), (c + step, c + step < frames)):

            @pl.when(valid)
            def _():
                pl.semaphore_signal(
                    barrier, inc=1, device_id={"frame": there}, device_id_type=MESH
                )

            expected = expected + jnp.where(valid, 1, 0)

    def rule_rows(j, valid, count):
        lane = lax.broadcasted_iota(jnp.int32, (count, TILE), 1)
        row = jnp.zeros((count, TILE), F32)
        for i in range(blocks):
            seen = mask_ref[i, j]
            if valid is not None:
                seen = seen * jnp.where(valid, 1, 0)
            row = jnp.where(lane == i, jnp.where(seen > 0, 0.0, BLOCKED), row)
        return row.astype(BF16)

    lane_at = lax.broadcasted_iota(jnp.int32, (TILE, TILE), 1)
    for i in range(blocks):
        qmark[i * TILE : (i + 1) * TILE, :] = jnp.where(lane_at == i, 1.0, 0.0).astype(BF16)
    near_tile, own_tile = (SINK + span) // TILE, (SINK + 2 * span) // TILE
    split = TILE + BATCH
    segments = [(own_tile + j, TILE, None) for j in range(blocks)]
    segments += [(near_tile, TILE, has_near), (near_tile + 1, BATCH, has_near)]
    segments += [(near_tile + 3, BATCH, has_near), (0, TILE, None)]
    segments += [(near_tile + 1, BATCH, has_near), (near_tile + 3, BATCH, has_near)]
    segments += [(near_tile + 2, TILE, has_near)]
    at = 0
    for j, count, valid in segments:
        kmark[at : at + count, :] = rule_rows(j, valid, count)
        at += count
    for j in range(blocks):
        far_rule[j * 16 : (j + 1) * 16, :] = rule_rows(SINK // TILE + j, None, 16)
    ones[...] = jnp.ones(ones.shape, BF16)

    pl.semaphore_wait(barrier, expected)

    def remote(src, dst, send, recv, device):
        return pltpu.make_async_remote_copy(
            src_ref=src,
            dst_ref=dst,
            send_sem=send,
            recv_sem=recv,
            device_id=device,
            device_id_type=MESH,
        )

    def place_of(half, k):
        if isinstance(k, int):
            low, high = (k, k + 2) if k < 2 else (k + 2, chunks + 1 - k)
            return jnp.where(half == 0, low, high)
        return jnp.where(
            half == 0, jnp.where(k < 2, k, k + 2), jnp.where(k < 2, k + 2, chunks + 1 - k)
        )

    def place(k):
        return place_of(h, k)

    def other_place(k):
        return place_of(1 - h, k)

    def chunk_rows(i):
        return pl.ds(pl.multiple_of(i * CHUNK, CHUNK), CHUNK)

    def near_copy(k):
        at = chunk_rows(place(k))
        return remote(
            own.at[at], near.at[at], send_near.at[k], recv_near.at[place(k)], {"frame": c + 1}
        )

    def x_copy(k):
        at = chunk_rows(place(k))
        return remote(
            near.at[at], near.at[at], send_x.at[k], recv_near.at[place(k)], {"head": 1 - h}
        )

    def x_arrival(k):
        at = chunk_rows(other_place(k))
        return remote(
            near.at[at], near.at[at], send_x.at[k], recv_near.at[other_place(k)], {"head": 1 - h}
        )

    def sink_place(p):
        return place(p) if p < PIECES else other_place(p - PIECES)

    def sink_z(p):
        i = sink_place(p)
        at = chunk_rows(i)
        return remote(sink.at[at], sink.at[at], send_sink.at[p], recv_sink.at[i], {"frame": c + 2})

    def sink_y(p):
        at = chunk_rows(place(p))
        return remote(
            sink.at[at],
            sink.at[at],
            send_sink.at[3 * PIECES + p],
            recv_sink.at[place(p)],
            {"frame": c + 1},
        )

    def sink_x(p, half):
        at = chunk_rows(place_of(half, p))
        return remote(
            sink.at[at],
            sink.at[at],
            send_sink.at[2 * PIECES + p],
            recv_sink.at[place_of(half, p)],
            {"head": 1 - h},
        )

    def block_rows(b):
        return pl.ds(pl.multiple_of(b * TILE, TILE), TILE)

    def q_copy(b):
        at = block_rows(b)
        return remote(qbuf.at[at], their_q.at[at], send_q.at[b], recv_q.at[b], {"frame": c - 2})

    def rule_copy():
        return remote(far_rule, their_rule, send_rule.at[0], recv_rule.at[0], {"frame": c - 2})

    def o_copy(b):
        at = block_rows(b)
        return remote(their_out.at[at], far_out.at[at], send_o.at[b], recv_o.at[b], {"frame": c + 2})

    def l_copy(b):
        return remote(
            their_lse.at[b, pl.ds(0, 8)],
            far_lse.at[b, pl.ds(0, 8)],
            send_l.at[b],
            recv_l.at[b],
            {"frame": c + 2},
        )

    def out_copy(b):
        return remote(outgoing.at[b], incoming.at[b], send_out.at[b], recv_out.at[b], {"head": 1 - h})

    def modulate(start, count):
        x = tok[pl.ds(start, count), :].astype(F32)
        mean_square = jnp.mean(x * x, axis=-1, keepdims=True)
        normed = x * lax.rsqrt(mean_square + 1e-06)
        scale_shift = table_ref[level_ref[start // FRAME_TOK]]
        return (normed * (1.0 + scale_shift[0:1]) + scale_shift[1:2]).astype(BF16)

    def batch_at(m):
        middle = (m >= 1) & (m <= chunks // 2 - 2)
        low = jnp.where(m == 0, 0, jnp.where(middle, m + 1, 1))
        high = jnp.where(m == 0, 1, jnp.where(middle, chunks // 2 - m, 0))
        return pl.multiple_of(jnp.where(h == 0, low, high) * BATCH, BATCH)

    def send_near_chunk(k, when):
        if k < DIRECT:

            @pl.when(gives_near & when)
            def _():
                near_copy(k).start()

    loads[0].wait()
    loads[7].wait()
    for m in range(AHEAD // 2):
        start = batch_at(m)
        own[pl.ds(start, BATCH), :] = modulate(start, BATCH)
        if m == 0:

            @pl.when(c == 0)
            def _():
                sink[pl.ds(start, BATCH), :] = own[pl.ds(start, BATCH), :]

            @pl.when((c == 0) & serves)
            def _():
                for p in range(PIECES):
                    sink_z(p).start()

        send_near_chunk(2 * m, c >= 0)
        send_near_chunk(2 * m + 1, c >= 0)

    @pl.when(c == 0)
    def _():
        start = pl.multiple_of((1 - h) * BATCH, BATCH)
        sink[pl.ds(start, BATCH), :] = modulate(start, BATCH)

        @pl.when(serves)
        def _():
            for p in range(PIECES, 2 * PIECES):
                sink_z(p).start()

    def rest(m, carry):
        start = batch_at(m)
        own[pl.ds(start, BATCH), :] = modulate(start, BATCH)
        return carry

    lax.fori_loop(AHEAD // 2, chunks // 2, rest, 0)
    for k in range(AHEAD, DIRECT):
        send_near_chunk(k, odd)

    def project(flat, weight, dst, start, scale=None):
        res = jnp.dot(flat, weight[...], preferred_element_type=F32)
        if scale is not None:
            res = res * scale
        dst[start : start + flat.shape[0], :] = res.astype(BF16)

    def near_point(k):
        @pl.when(has_near)
        def _():
            near_copy(k).wait_recv()
            if k < relays:
                x_copy(k).start()

        send_near_chunk(k + AHEAD, even)

    def sink_even(p, lo, hi):
        @pl.when(even & (c >= 2 * lo) & (c < 2 * hi))
        def _():
            sink_z(p).wait_recv()

            @pl.when(serves)
            def _():
                sink_z(p).start()

            if p < PIECES:
                sink_y(p).start()

    def sink_odd(p, lo, hi):
        @pl.when(odd & (c >= 2 * lo) & (c < 2 * hi))
        def _():
            sink_y(p).wait_recv()
            sink_x(p, h).start()

    def head_cols(n):
        return slice(n * HEAD_DIM, (n + 1) * HEAD_DIM)

    def score(q_ref, q_at, q_stop, k_at, k_stop, mark, mark_at, n):
        left = jnp.concatenate([q_ref[q_at:q_stop, head_cols(n)], qmark[q_at:q_stop, :]], axis=1)
        marks = mark[mark_at : mark_at + k_stop - k_at, :]
        right = jnp.concatenate([kbuf[k_at:k_stop, head_cols(n)], marks], axis=1)
        return lax.dot_general(left, right, (((1,), (1,)), ((), ())), preferred_element_type=F32)

    def mix(num, k_at, k_stop, n):
        right = jnp.concatenate(
            [vbuf[k_at:k_stop, head_cols(n)], ones[0 : k_stop - k_at, :]], axis=1
        )
        both = jnp.dot(num.astype(BF16), right, preferred_element_type=F32)
        return both[:, :HEAD_DIM], both[:, HEAD_DIM:]

    def wide(column, shape):
        return jnp.broadcast_to(column, shape)

    loads[1].wait()
    project(own[...], wq, qbuf, 0, 1.0 / math.sqrt(HEAD_DIM))

    @pl.when(has_far)
    def _():
        rule_copy().start()
        for b in range(blocks):
            q_copy(b).start()

    near_point(0)
    sink_even(0, 1, 2)
    loads[2].wait()
    project(own[...], wk, kbuf, 0)
    loads[3].wait()
    project(own[...], wv, vbuf, 0)

    def own_heads(lo, hi):
        for n in range(lo, hi):
            scores = score(qbuf, 0, span, 0, span, kmark, 0, n)
            peak = jnp.max(scores, axis=-1, keepdims=True)
            rows_out, total = mix(jnp.exp(scores - peak), 0, span, n)
            peak_buf[:, head_cols(n)] = wide(peak, total.shape)
            total_buf[:, head_cols(n)] = total
            mixed_buf[:, head_cols(n)] = rows_out

    sink_even(1, 1, 2)
    own_heads(0, heads // 2)
    near_point(1)
    sink_even(2, 1, 2)
    sink_even(0, 2, 3)
    own_heads(heads // 2, heads)
    near_point(2)
    sink_even(3, 1, 2)
    sink_even(1, 2, 3)
    sink_odd(0, 1, 2)
    near_point(3)
    sink_even(2, 2, 3)
    sink_even(0, 3, frames)
    sink_odd(1, 1, 2)

    def serve(g):
        lo, hi = g * half_rows, (g + 1) * half_rows

        @pl.when(serves)
        def _():
            if g == 0:
                rule_copy().wait_recv()
                for j in range(blocks):
                    small = their_rule[j * 16 : (j + 1) * 16, :]
                    their_mark[j * TILE : (j + 1) * TILE, :] = jnp.concatenate(
                        [small] * (TILE // 16), axis=0
                    )
            for b in range(g * half_blocks, (g + 1) * half_blocks):
                q_copy(b).wait_recv()
            lanes = lax.broadcasted_iota(jnp.int32, (half_rows, HEAD_DIM), 1)
            lse_all = jnp.zeros((half_rows, HEAD_DIM), F32)
            for n in range(heads):
                scores = score(their_q, lo, hi, 0, span, their_mark, 0, n)
                peak = jnp.max(scores, axis=-1, keepdims=True)
                rows_out, total = mix(jnp.exp(scores - peak), 0, span, n)
                their_out[lo:hi, head_cols(n)] = (rows_out / total).astype(BF16)
                lse_all = jnp.where(lanes == n, peak + jnp.log(total), lse_all)
            for b in range(half_blocks):
                their_lse[g * half_blocks + b] = lse_all[b * TILE : (b + 1) * TILE, :].T
            for b in range(g * half_blocks, (g + 1) * half_blocks):
                l_copy(b).start()
                o_copy(b).start()

    near_point(4)
    sink_even(3, 2, 3)
    sink_even(1, 3, frames)
    sink_odd(0, 2, 3)

    @pl.when(has_near)
    def _():
        for k in range(EARLY):
            x_arrival(k).wait_recv()
        flat = jnp.concatenate([near[0:split, :], near[span - BATCH : span, :]], axis=0)
        project(flat, wk, kbuf, first_at)
        project(flat, wv, vbuf, first_at)

    @pl.when(jnp.logical_not(has_near))
    def _():
        for buf in (kbuf, vbuf):
            buf[first_at:sink_at, :] = jnp.zeros((half_rows, local), BF16)
            buf[last_at:keys_end, :] = jnp.zeros((half_rows, local), BF16)

    near_point(5)
    sink_even(2, 3, frames)
    sink_odd(1, 2, 3)
    near_point(6)
    sink_even(3, 3, frames)
    sink_odd(0, 3, frames)
    serve(0)
    sink_odd(1, 3, frames)

    def project_sink():
        project(sink[...], wk, kbuf, sink_at)
        project(sink[...], wv, vbuf, sink_at)

    for n in range(heads):
        scores = score(qbuf, 0, span, first_at, sink_at, kmark, first_at, n)
        before = peak_buf[:, head_cols(n)]
        peak = jnp.maximum(jnp.max(scores, axis=-1, keepdims=True), before)
        keep = jnp.exp(before - peak)
        spread = jnp.concatenate([peak] * (scores.shape[1] // HEAD_DIM), axis=1)
        rows_out, total = mix(jnp.exp(scores - spread), first_at, sink_at, n)
        peak_buf[:, head_cols(n)] = peak
        total_buf[:, head_cols(n)] = total_buf[:, head_cols(n)] * keep + total
        mixed_buf[:, head_cols(n)] = mixed_buf[:, head_cols(n)] * keep + rows_out

    for i in (4, 5, 6):
        loads[i].wait()

    tail_at = keys_end - TILE

    @pl.when(has_near)
    def _():
        for k in range(EARLY, EARLY + 2):
            x_arrival(k).wait_recv()
        flat = jnp.concatenate(
            [near[split : split + BATCH, :], near[span - 2 * BATCH : span - BATCH, :]], axis=0
        )
        project(flat, wk, kbuf, last_at)
        project(flat, wv, vbuf, last_at)

    @pl.when(has_far & odd)
    def _():
        for p in range(PIECES):
            sink_x(p, 1 - h).wait_recv()

    @pl.when(c == 1)
    def _():
        sink[...] = near[0:SINK, :]

    project_sink()

    @pl.when(has_near)
    def _():
        for k in range(relays, DIRECT):
            near_copy(k).wait_recv()
        for k in range(EARLY + 2, relays):
            x_arrival(k).wait_recv()
        flat = near[split + BATCH : span - 2 * BATCH, :]
        project(flat, wk, kbuf, tail_at)
        project(flat, wv, vbuf, tail_at)

    @pl.when(jnp.logical_not(has_far))
    def _():
        far_out[...] = jnp.zeros(far_out.shape, BF16)
        far_lse[...] = jnp.full(far_lse.shape, BLOCKED, F32)

    def last_keys(g):
        lo, hi = g * half_rows, (g + 1) * half_rows
        for n in range(heads):
            scores = score(qbuf, lo, hi, sink_at, keys_end, kmark, sink_at, n)
            before = peak_buf[lo:hi, head_cols(n)]
            peak = jnp.maximum(jnp.max(scores, axis=-1, keepdims=True), before)
            keep = jnp.exp(before - peak)
            spread = jnp.concatenate([peak] * (scores.shape[1] // HEAD_DIM), axis=1)
            rows_out, total = mix(jnp.exp(scores - spread), sink_at, keys_end, n)
            peak_buf[lo:hi, head_cols(n)] = peak
            total_buf[lo:hi, head_cols(n)] = total_buf[lo:hi, head_cols(n)] * keep + total
            mixed_buf[lo:hi, head_cols(n)] = mixed_buf[lo:hi, head_cols(n)] * keep + rows_out

    def send_block(b):
        lo, hi = b * TILE, (b + 1) * TILE

        @pl.when(has_far)
        def _():
            l_copy(b).wait_recv()
            o_copy(b).wait_recv()

        far_cols = far_lse[b].T
        parts = []
        for n in range(heads):
            before = peak_buf[lo:hi, head_cols(n)]
            far_peak = wide(far_cols[:, n : n + 1], before.shape)
            peak = jnp.maximum(before, far_peak)
            keep = jnp.exp(before - peak)
            far_weight = jnp.exp(far_peak - peak)
            total = total_buf[lo:hi, head_cols(n)] * keep + far_weight
            rows_out = (
                mixed_buf[lo:hi, head_cols(n)] * keep
                + far_out[lo:hi, head_cols(n)].astype(F32) * far_weight
            )
            parts.append((rows_out / total).astype(BF16))
        attended = jnp.concatenate(parts, axis=1)
        outgoing[b] = jnp.dot(attended, wo_theirs[...], preferred_element_type=F32).astype(BF16)
        out_copy(b).start()
        return attended

    def keep_block(b, attended):
        lo, hi = b * TILE, (b + 1) * TILE
        kept[lo:hi, :] = resid[lo:hi, :].astype(F32) + jnp.dot(
            attended, wo_mine[...], preferred_element_type=F32
        )

    last_keys(0)
    first = send_block(0)
    serve(1)
    second = send_block(1)
    keep_block(0, first)
    last_keys(1)
    keep_block(1, second)
    for b in range(half_blocks, blocks):
        keep_block(b, send_block(b))

    def store(b):
        at = pl.ds(b * TILE, TILE)
        return pltpu.make_async_copy(done.at[at], out_hbm.at[at], store_sem.at[b])

    for b in range(blocks):
        at = slice(b * TILE, (b + 1) * TILE)
        out_copy(b).wait_recv()
        done[at, :] = (kept[at, :] + incoming[b].astype(F32)).astype(BF16)
        store(b).start()

    for b in range(blocks):
        out_copy(b).wait_send()

    @pl.when(gives_near)
    def _():
        for k in range(DIRECT):
            near_copy(k).wait_send()

    @pl.when(has_near)
    def _():
        for k in range(relays):
            x_copy(k).wait_send()

    @pl.when(serves & even)
    def _():
        for p in range(2 * PIECES):
            sink_z(p).wait_send()

    @pl.when(serves)
    def _():
        for b in range(blocks):
            o_copy(b).wait_send()
            l_copy(b).wait_send()

    @pl.when(has_far & odd)
    def _():
        for p in range(PIECES):
            sink_x(p, h).wait_send()

    @pl.when(has_far & even)
    def _():
        for p in range(PIECES):
            sink_y(p).wait_send()

    @pl.when(has_far)
    def _():
        rule_copy().wait_send()
        for b in range(blocks):
            q_copy(b).wait_send()

    for b in range(blocks):
        store(b).wait()


def shards(
    tokens, query_weight, key_weight, value_weight, out_weight, block_mask, frame_level, modulation
):
    span, width = tokens.shape
    local = query_weight.shape[1]
    share = width // lax.axis_size("head")
    chunks = span // CHUNK
    relays = chunks - DIRECT
    blocks = span // TILE
    keys = SINK + 2 * span
    dma = pltpu.SemaphoreType.DMA
    anywhere = pl.BlockSpec(memory_space=pl.ANY)
    smem = pl.BlockSpec(memory_space=pltpu.SMEM)
    return pl.pallas_call(
        functools.partial(layer_kernel, lax.axis_size("frame")),
        out_shape=jax.ShapeDtypeStruct((span, share), BF16),
        in_specs=[anywhere] * 5 + [smem, smem, anywhere],
        out_specs=anywhere,
        scratch_shapes=[
            pltpu.VMEM(modulation.shape, F32),
            pltpu.VMEM((span, share), BF16),
            pltpu.VMEM((span, width), BF16),
            pltpu.VMEM((span, share), BF16),
            pltpu.VMEM((width, local), BF16),
            pltpu.VMEM((width, local), BF16),
            pltpu.VMEM((width, local), BF16),
            pltpu.VMEM((local, share), BF16),
            pltpu.VMEM((local, share), BF16),
            pltpu.VMEM((span, width), BF16),
            pltpu.VMEM((span, width), BF16),
            pltpu.VMEM((SINK, width), BF16),
            pltpu.VMEM((span, local), BF16),
            pltpu.VMEM((keys, local), BF16),
            pltpu.VMEM((keys, local), BF16),
            pltpu.VMEM((span, TILE), BF16),
            pltpu.VMEM((keys, TILE), BF16),
            pltpu.VMEM((span, TILE), BF16),
            pltpu.VMEM((blocks * 16, TILE), BF16),
            pltpu.VMEM((blocks * 16, TILE), BF16),
            pltpu.VMEM((span, TILE), BF16),
            pltpu.VMEM((span, local), BF16),
            pltpu.VMEM((span, local), BF16),
            pltpu.VMEM((blocks, TILE, TILE), F32),
            pltpu.VMEM((span, local), BF16),
            pltpu.VMEM((blocks, TILE, TILE), F32),
            pltpu.VMEM((span, local), F32),
            pltpu.VMEM((span, local), F32),
            pltpu.VMEM((span, local), F32),
            pltpu.VMEM((blocks, TILE, share), BF16),
            pltpu.VMEM((blocks, TILE, share), BF16),
            pltpu.VMEM((span, share), F32),
            dma((8,)),
            dma((blocks,)),
            dma((DIRECT,)),
            dma((relays,)),
            dma((chunks,)),
            dma((4 * PIECES,)),
            dma((2 * PIECES,)),
            dma((blocks,)),
            dma((blocks,)),
            dma((1,)),
            dma((1,)),
            dma((blocks,)),
            dma((blocks,)),
            dma((blocks,)),
            dma((blocks,)),
            dma((blocks,)),
            dma((blocks,)),
        ],
        compiler_params=pltpu.CompilerParams(
            collective_id=0, has_side_effects=True, vmem_limit_bytes=60 * 1024 * 1024
        ),
        name="layer",
    )(
        tokens,
        query_weight,
        key_weight,
        value_weight,
        out_weight,
        block_mask[0],
        frame_level,
        modulation,
    )


def solution(mesh):
    placed = (
        P(("batch", "frame"), None),
        P(None, "head"),
        P(None, "head"),
        P(None, "head"),
        P("head", None),
        P(("batch", "frame"), None, None),
        P(("batch", "frame")),
        P(),
    )
    return jax.shard_map(
        shards, mesh=mesh, in_specs=placed, out_specs=P(("batch", "frame"), "head"), check_vma=False
    )
```

```python
import functools
import math

import jax
import jax.numpy as jnp
from jax import lax
from jax.experimental import pallas as pl
from jax.experimental.pallas import tpu as pltpu
from jax.sharding import PartitionSpec as P

HEAD_DIM = 128
FRAME_TOK = 128
SINK = 128
TILE = 128
CHUNK = 32
DIRECT = 9
EARLY = 4
AHEAD = 2
BATCH = 2 * CHUNK
PIECES = 2
BLOCKED = -1e30
MESH = pl.DeviceIdType.MESH
BF16, F32 = jnp.bfloat16, jnp.float32


def layer_kernel(
    frames,
    tok_hbm,
    wq_hbm,
    wk_hbm,
    wv_hbm,
    wo_hbm,
    mask_ref,
    level_ref,
    table_hbm,
    done,
    table_ref,
    tok,
    resid,
    wq,
    wk,
    wv,
    wo_mine,
    wo_theirs,
    own,
    near,
    sink,
    qbuf,
    kbuf,
    vbuf,
    qmark,
    kmark,
    ones,
    far_rule,
    their_rule,
    their_mark,
    their_q,
    their_out,
    their_lse,
    far_out,
    far_lse,
    peak_buf,
    total_buf,
    mixed_buf,
    outgoing,
    incoming,
    kept,
    load_sem,
    send_near,
    send_x,
    recv_near,
    send_sink,
    recv_sink,
    send_q,
    recv_q,
    send_rule,
    recv_rule,
    send_o,
    recv_o,
    send_l,
    recv_l,
    send_out,
    recv_out,
):
    c = lax.axis_index("frame")
    h = lax.axis_index("head")
    span, width = own.shape
    local = wq.shape[1]
    share = done.shape[1]
    heads = local // HEAD_DIM
    blocks = span // TILE
    chunks = span // CHUNK
    relays = chunks - DIRECT
    half_rows = span // 2
    half_blocks = blocks // 2
    first_at, sink_at, last_at = span, span + half_rows, span + half_rows + SINK
    keys_end = kbuf.shape[0]

    has_near, gives_near = c >= 1, c + 1 < frames
    has_far, serves = c >= 2, c + 2 < frames
    odd, even = c % 2 == 1, c % 2 == 0

    def load(src, dst, i):
        return pltpu.make_async_copy(src, dst, load_sem.at[i])

    my_cols = pl.ds(pl.multiple_of(h * share, share), share)
    their_cols = pl.ds(pl.multiple_of((1 - h) * share, share), share)
    loads = [
        load(tok_hbm, tok, 0),
        load(wq_hbm, wq, 1),
        load(wk_hbm, wk, 2),
        load(wv_hbm, wv, 3),
        load(wo_hbm.at[:, their_cols], wo_theirs, 4),
        load(wo_hbm.at[:, my_cols], wo_mine, 5),
        load(tok_hbm.at[:, my_cols], resid, 6),
        load(table_hbm, table_ref, 7),
    ]
    for i in (0, 7, 1, 2, 3, 4, 5, 6):
        loads[i].start()

    barrier = pltpu.get_barrier_semaphore()
    pl.semaphore_signal(barrier, inc=1, device_id={"head": 1 - h}, device_id_type=MESH)
    expected = 1
    for step in (1, 2):
        for there, valid in ((c - step, c >= step), (c + step, c + step < frames)):

            @pl.when(valid)
            def _():
                pl.semaphore_signal(
                    barrier, inc=1, device_id={"frame": there}, device_id_type=MESH
                )

            expected = expected + jnp.where(valid, 1, 0)

    def rule_rows(j, valid, count):
        lane = lax.broadcasted_iota(jnp.int32, (count, TILE), 1)
        row = jnp.zeros((count, TILE), F32)
        for i in range(blocks):
            seen = mask_ref[i, j]
            if valid is not None:
                seen = seen * jnp.where(valid, 1, 0)
            row = jnp.where(lane == i, jnp.where(seen > 0, 0.0, BLOCKED), row)
        return row.astype(BF16)

    lane_at = lax.broadcasted_iota(jnp.int32, (TILE, TILE), 1)
    for i in range(blocks):
        qmark[i * TILE : (i + 1) * TILE, :] = jnp.where(lane_at == i, 1.0, 0.0).astype(BF16)
    near_tile, own_tile = (SINK + span) // TILE, (SINK + 2 * span) // TILE
    split = TILE + BATCH
    segments = [(own_tile + j, TILE, None) for j in range(blocks)]
    segments += [(near_tile, TILE, has_near), (near_tile + 1, BATCH, has_near)]
    segments += [(near_tile + 3, BATCH, has_near), (0, TILE, None)]
    segments += [(near_tile + 1, BATCH, has_near), (near_tile + 3, BATCH, has_near)]
    segments += [(near_tile + 2, TILE, has_near)]
    at = 0
    for j, count, valid in segments:
        kmark[at : at + count, :] = rule_rows(j, valid, count)
        at += count
    for j in range(blocks):
        far_rule[j * 16 : (j + 1) * 16, :] = rule_rows(SINK // TILE + j, None, 16)
    ones[...] = jnp.ones(ones.shape, BF16)

    pl.semaphore_wait(barrier, expected)

    def remote(src, dst, send, recv, device):
        return pltpu.make_async_remote_copy(
            src_ref=src,
            dst_ref=dst,
            send_sem=send,
            recv_sem=recv,
            device_id=device,
            device_id_type=MESH,
        )

    def place_of(half, k):
        if isinstance(k, int):
            low, high = (k, k + 2) if k < 2 else (k + 2, chunks + 1 - k)
            return jnp.where(half == 0, low, high)
        return jnp.where(
            half == 0, jnp.where(k < 2, k, k + 2), jnp.where(k < 2, k + 2, chunks + 1 - k)
        )

    def place(k):
        return place_of(h, k)

    def other_place(k):
        return place_of(1 - h, k)

    def chunk_rows(i):
        return pl.ds(pl.multiple_of(i * CHUNK, CHUNK), CHUNK)

    def near_copy(k):
        at = chunk_rows(place(k))
        return remote(
            own.at[at], near.at[at], send_near.at[k], recv_near.at[place(k)], {"frame": c + 1}
        )

    def x_copy(k):
        at = chunk_rows(place(k))
        return remote(
            near.at[at], near.at[at], send_x.at[k], recv_near.at[place(k)], {"head": 1 - h}
        )

    def x_arrival(k):
        at = chunk_rows(other_place(k))
        return remote(
            near.at[at], near.at[at], send_x.at[k], recv_near.at[other_place(k)], {"head": 1 - h}
        )

    def sink_place(p):
        return place(p) if p < PIECES else other_place(p - PIECES)

    def sink_z(p):
        i = sink_place(p)
        at = chunk_rows(i)
        return remote(sink.at[at], sink.at[at], send_sink.at[p], recv_sink.at[i], {"frame": c + 2})

    def sink_y(p):
        at = chunk_rows(place(p))
        return remote(
            sink.at[at],
            sink.at[at],
            send_sink.at[3 * PIECES + p],
            recv_sink.at[place(p)],
            {"frame": c + 1},
        )

    def sink_x(p, half):
        at = chunk_rows(place_of(half, p))
        return remote(
            sink.at[at],
            sink.at[at],
            send_sink.at[2 * PIECES + p],
            recv_sink.at[place_of(half, p)],
            {"head": 1 - h},
        )

    def block_rows(b):
        return pl.ds(pl.multiple_of(b * TILE, TILE), TILE)

    def q_copy(b):
        at = block_rows(b)
        return remote(qbuf.at[at], their_q.at[at], send_q.at[b], recv_q.at[b], {"frame": c - 2})

    def rule_copy():
        return remote(far_rule, their_rule, send_rule.at[0], recv_rule.at[0], {"frame": c - 2})

    def o_copy(b):
        at = block_rows(b)
        return remote(their_out.at[at], far_out.at[at], send_o.at[b], recv_o.at[b], {"frame": c + 2})

    def l_copy(b):
        return remote(
            their_lse.at[b, pl.ds(0, 8)],
            far_lse.at[b, pl.ds(0, 8)],
            send_l.at[b],
            recv_l.at[b],
            {"frame": c + 2},
        )

    def out_copy(b):
        return remote(outgoing.at[b], incoming.at[b], send_out.at[b], recv_out.at[b], {"head": 1 - h})

    def modulate(start, count):
        x = tok[pl.ds(start, count), :].astype(F32)
        mean_square = jnp.mean(x * x, axis=-1, keepdims=True)
        normed = x * lax.rsqrt(mean_square + 1e-06)
        scale_shift = table_ref[level_ref[start // FRAME_TOK]]
        return (normed * (1.0 + scale_shift[0:1]) + scale_shift[1:2]).astype(BF16)

    def batch_at(m):
        middle = (m >= 1) & (m <= chunks // 2 - 2)
        low = jnp.where(m == 0, 0, jnp.where(middle, m + 1, 1))
        high = jnp.where(m == 0, 1, jnp.where(middle, chunks // 2 - m, 0))
        return pl.multiple_of(jnp.where(h == 0, low, high) * BATCH, BATCH)

    def send_near_chunk(k, when):
        if k < DIRECT:

            @pl.when(gives_near & when)
            def _():
                near_copy(k).start()

    loads[0].wait()
    loads[7].wait()
    for m in range(AHEAD // 2):
        start = batch_at(m)
        own[pl.ds(start, BATCH), :] = modulate(start, BATCH)
        if m == 0:

            @pl.when(c == 0)
            def _():
                sink[pl.ds(start, BATCH), :] = own[pl.ds(start, BATCH), :]

            @pl.when((c == 0) & serves)
            def _():
                for p in range(PIECES):
                    sink_z(p).start()

        send_near_chunk(2 * m, c >= 0)
        send_near_chunk(2 * m + 1, c >= 0)

    @pl.when(c == 0)
    def _():
        start = pl.multiple_of((1 - h) * BATCH, BATCH)
        sink[pl.ds(start, BATCH), :] = modulate(start, BATCH)

        @pl.when(serves)
        def _():
            for p in range(PIECES, 2 * PIECES):
                sink_z(p).start()

    def rest(m, carry):
        start = batch_at(m)
        own[pl.ds(start, BATCH), :] = modulate(start, BATCH)
        return carry

    lax.fori_loop(AHEAD // 2, chunks // 2, rest, 0)
    for k in range(AHEAD, DIRECT):
        send_near_chunk(k, odd)

    def project(flat, weight, dst, start, scale=None):
        res = jnp.dot(flat, weight[...], preferred_element_type=F32)
        if scale is not None:
            res = res * scale
        dst[start : start + flat.shape[0], :] = res.astype(BF16)

    def near_point(k):
        @pl.when(has_near)
        def _():
            near_copy(k).wait_recv()
            if k < relays:
                x_copy(k).start()

        send_near_chunk(k + AHEAD, even)

    def sink_even(p, lo, hi):
        @pl.when(even & (c >= 2 * lo) & (c < 2 * hi))
        def _():
            sink_z(p).wait_recv()

            @pl.when(serves)
            def _():
                sink_z(p).start()

            if p < PIECES:
                sink_y(p).start()

    def sink_odd(p, lo, hi):
        @pl.when(odd & (c >= 2 * lo) & (c < 2 * hi))
        def _():
            sink_y(p).wait_recv()
            sink_x(p, h).start()

    def head_cols(n):
        return slice(n * HEAD_DIM, (n + 1) * HEAD_DIM)

    def score(q_ref, q_at, q_stop, k_at, k_stop, mark, mark_at, n):
        left = jnp.concatenate([q_ref[q_at:q_stop, head_cols(n)], qmark[q_at:q_stop, :]], axis=1)
        marks = mark[mark_at : mark_at + k_stop - k_at, :]
        right = jnp.concatenate([kbuf[k_at:k_stop, head_cols(n)], marks], axis=1)
        return lax.dot_general(left, right, (((1,), (1,)), ((), ())), preferred_element_type=F32)

    def mix(num, k_at, k_stop, n):
        right = jnp.concatenate(
            [vbuf[k_at:k_stop, head_cols(n)], ones[0 : k_stop - k_at, :]], axis=1
        )
        both = jnp.dot(num.astype(BF16), right, preferred_element_type=F32)
        return both[:, :HEAD_DIM], both[:, HEAD_DIM:]

    def wide(column, shape):
        return jnp.broadcast_to(column, shape)

    loads[1].wait()
    project(own[...], wq, qbuf, 0, 1.0 / math.sqrt(HEAD_DIM))

    @pl.when(has_far)
    def _():
        rule_copy().start()
        for b in range(blocks):
            q_copy(b).start()

    near_point(0)
    sink_even(0, 1, 2)
    loads[2].wait()
    project(own[...], wk, kbuf, 0)
    loads[3].wait()
    project(own[...], wv, vbuf, 0)

    def own_heads(lo, hi):
        for n in range(lo, hi):
            scores = score(qbuf, 0, span, 0, span, kmark, 0, n)
            peak = jnp.max(scores, axis=-1, keepdims=True)
            rows_out, total = mix(jnp.exp(scores - peak), 0, span, n)
            peak_buf[:, head_cols(n)] = wide(peak, total.shape)
            total_buf[:, head_cols(n)] = total
            mixed_buf[:, head_cols(n)] = rows_out

    sink_even(1, 1, 2)
    own_heads(0, heads // 2)
    near_point(1)
    sink_even(2, 1, 2)
    sink_even(0, 2, 3)
    own_heads(heads // 2, heads)
    near_point(2)
    sink_even(3, 1, 2)
    sink_even(1, 2, 3)
    sink_odd(0, 1, 2)
    near_point(3)
    sink_even(2, 2, 3)
    sink_even(0, 3, frames)
    sink_odd(1, 1, 2)

    def serve(g):
        lo, hi = g * half_rows, (g + 1) * half_rows

        @pl.when(serves)
        def _():
            if g == 0:
                rule_copy().wait_recv()
                for j in range(blocks):
                    small = their_rule[j * 16 : (j + 1) * 16, :]
                    their_mark[j * TILE : (j + 1) * TILE, :] = jnp.concatenate(
                        [small] * (TILE // 16), axis=0
                    )
            for b in range(g * half_blocks, (g + 1) * half_blocks):
                q_copy(b).wait_recv()
            lanes = lax.broadcasted_iota(jnp.int32, (half_rows, HEAD_DIM), 1)
            lse_all = jnp.zeros((half_rows, HEAD_DIM), F32)
            for n in range(heads):
                scores = score(their_q, lo, hi, 0, span, their_mark, 0, n)
                peak = jnp.max(scores, axis=-1, keepdims=True)
                rows_out, total = mix(jnp.exp(scores - peak), 0, span, n)
                their_out[lo:hi, head_cols(n)] = (rows_out / total).astype(BF16)
                lse_all = jnp.where(lanes == n, peak + jnp.log(total), lse_all)
            for b in range(half_blocks):
                their_lse[g * half_blocks + b] = lse_all[b * TILE : (b + 1) * TILE, :].T
            for b in range(g * half_blocks, (g + 1) * half_blocks):
                l_copy(b).start()
                o_copy(b).start()

    near_point(4)
    sink_even(3, 2, 3)
    sink_even(1, 3, frames)
    sink_odd(0, 2, 3)

    @pl.when(has_near)
    def _():
        for k in range(EARLY):
            x_arrival(k).wait_recv()
        flat = jnp.concatenate([near[0:split, :], near[span - BATCH : span, :]], axis=0)
        project(flat, wk, kbuf, first_at)
        project(flat, wv, vbuf, first_at)

    @pl.when(jnp.logical_not(has_near))
    def _():
        for buf in (kbuf, vbuf):
            buf[first_at:sink_at, :] = jnp.zeros((half_rows, local), BF16)
            buf[last_at:keys_end, :] = jnp.zeros((half_rows, local), BF16)

    near_point(5)
    sink_even(2, 3, frames)
    sink_odd(1, 2, 3)
    near_point(6)
    sink_even(3, 3, frames)
    sink_odd(0, 3, frames)
    serve(0)
    sink_odd(1, 3, frames)

    def project_sink():
        project(sink[...], wk, kbuf, sink_at)
        project(sink[...], wv, vbuf, sink_at)

    for n in range(heads):
        scores = score(qbuf, 0, span, first_at, sink_at, kmark, first_at, n)
        before = peak_buf[:, head_cols(n)]
        peak = jnp.maximum(jnp.max(scores, axis=-1, keepdims=True), before)
        keep = jnp.exp(before - peak)
        spread = jnp.concatenate([peak] * (scores.shape[1] // HEAD_DIM), axis=1)
        rows_out, total = mix(jnp.exp(scores - spread), first_at, sink_at, n)
        peak_buf[:, head_cols(n)] = peak
        total_buf[:, head_cols(n)] = total_buf[:, head_cols(n)] * keep + total
        mixed_buf[:, head_cols(n)] = mixed_buf[:, head_cols(n)] * keep + rows_out

    for i in (4, 5, 6):
        loads[i].wait()

    tail_at = keys_end - TILE

    @pl.when(has_near)
    def _():
        for k in range(EARLY, EARLY + 2):
            x_arrival(k).wait_recv()
        flat = jnp.concatenate(
            [near[split : split + BATCH, :], near[span - 2 * BATCH : span - BATCH, :]], axis=0
        )
        project(flat, wk, kbuf, last_at)
        project(flat, wv, vbuf, last_at)

    @pl.when(has_far & odd)
    def _():
        for p in range(PIECES):
            sink_x(p, 1 - h).wait_recv()

    @pl.when(c == 1)
    def _():
        sink[...] = near[0:SINK, :]

    project_sink()

    @pl.when(has_near)
    def _():
        for k in range(relays, DIRECT):
            near_copy(k).wait_recv()
        for k in range(EARLY + 2, relays):
            x_arrival(k).wait_recv()
        flat = near[split + BATCH : span - 2 * BATCH, :]
        project(flat, wk, kbuf, tail_at)
        project(flat, wv, vbuf, tail_at)

    @pl.when(jnp.logical_not(has_far))
    def _():
        far_out[...] = jnp.zeros(far_out.shape, BF16)
        far_lse[...] = jnp.full(far_lse.shape, BLOCKED, F32)

    def last_keys(g):
        lo, hi = g * half_rows, (g + 1) * half_rows
        for n in range(heads):
            scores = score(qbuf, lo, hi, sink_at, keys_end, kmark, sink_at, n)
            before = peak_buf[lo:hi, head_cols(n)]
            peak = jnp.maximum(jnp.max(scores, axis=-1, keepdims=True), before)
            keep = jnp.exp(before - peak)
            spread = jnp.concatenate([peak] * (scores.shape[1] // HEAD_DIM), axis=1)
            rows_out, total = mix(jnp.exp(scores - spread), sink_at, keys_end, n)
            peak_buf[lo:hi, head_cols(n)] = peak
            total_buf[lo:hi, head_cols(n)] = total_buf[lo:hi, head_cols(n)] * keep + total
            mixed_buf[lo:hi, head_cols(n)] = mixed_buf[lo:hi, head_cols(n)] * keep + rows_out

    def send_block(b):
        lo, hi = b * TILE, (b + 1) * TILE

        @pl.when(has_far)
        def _():
            l_copy(b).wait_recv()
            o_copy(b).wait_recv()

        far_cols = far_lse[b].T
        parts = []
        for n in range(heads):
            before = peak_buf[lo:hi, head_cols(n)]
            far_peak = wide(far_cols[:, n : n + 1], before.shape)
            peak = jnp.maximum(before, far_peak)
            keep = jnp.exp(before - peak)
            far_weight = jnp.exp(far_peak - peak)
            total = total_buf[lo:hi, head_cols(n)] * keep + far_weight
            rows_out = (
                mixed_buf[lo:hi, head_cols(n)] * keep
                + far_out[lo:hi, head_cols(n)].astype(F32) * far_weight
            )
            parts.append((rows_out / total).astype(BF16))
        attended = jnp.concatenate(parts, axis=1)
        outgoing[b] = jnp.dot(attended, wo_theirs[...], preferred_element_type=F32).astype(BF16)
        out_copy(b).start()
        return attended

    def keep_block(b, attended):
        lo, hi = b * TILE, (b + 1) * TILE
        kept[lo:hi, :] = resid[lo:hi, :].astype(F32) + jnp.dot(
            attended, wo_mine[...], preferred_element_type=F32
        )

    last_keys(0)
    first = send_block(0)
    serve(1)
    second = send_block(1)
    keep_block(0, first)
    last_keys(1)
    keep_block(1, second)
    for b in range(half_blocks, blocks):
        keep_block(b, send_block(b))

    for b in range(blocks):
        at = slice(b * TILE, (b + 1) * TILE)
        out_copy(b).wait_recv()
        done[at, :] = (kept[at, :] + incoming[b].astype(F32)).astype(BF16)

    for b in range(blocks):
        out_copy(b).wait_send()

    @pl.when(gives_near)
    def _():
        for k in range(DIRECT):
            near_copy(k).wait_send()

    @pl.when(has_near)
    def _():
        for k in range(relays):
            x_copy(k).wait_send()

    @pl.when(serves & even)
    def _():
        for p in range(2 * PIECES):
            sink_z(p).wait_send()

    @pl.when(serves)
    def _():
        for b in range(blocks):
            o_copy(b).wait_send()
            l_copy(b).wait_send()

    @pl.when(has_far & odd)
    def _():
        for p in range(PIECES):
            sink_x(p, h).wait_send()

    @pl.when(has_far & even)
    def _():
        for p in range(PIECES):
            sink_y(p).wait_send()

    @pl.when(has_far)
    def _():
        rule_copy().wait_send()
        for b in range(blocks):
            q_copy(b).wait_send()


def shards(
    tokens, query_weight, key_weight, value_weight, out_weight, block_mask, frame_level, modulation
):
    span, width = tokens.shape
    local = query_weight.shape[1]
    share = width // lax.axis_size("head")
    chunks = span // CHUNK
    relays = chunks - DIRECT
    blocks = span // TILE
    keys = SINK + 2 * span
    dma = pltpu.SemaphoreType.DMA
    anywhere = pl.BlockSpec(memory_space=pl.ANY)
    smem = pl.BlockSpec(memory_space=pltpu.SMEM)
    return pl.pallas_call(
        functools.partial(layer_kernel, lax.axis_size("frame")),
        out_shape=pltpu.VMEM((span, share), BF16),
        in_specs=[anywhere] * 5 + [smem, smem, anywhere],
        out_specs=pl.BlockSpec(memory_space=pltpu.VMEM),
        scratch_shapes=[
            pltpu.VMEM(modulation.shape, F32),
            pltpu.VMEM((span, width), BF16),
            pltpu.VMEM((span, share), BF16),
            pltpu.VMEM((width, local), BF16),
            pltpu.VMEM((width, local), BF16),
            pltpu.VMEM((width, local), BF16),
            pltpu.VMEM((local, share), BF16),
            pltpu.VMEM((local, share), BF16),
            pltpu.VMEM((span, width), BF16),
            pltpu.VMEM((span, width), BF16),
            pltpu.VMEM((SINK, width), BF16),
            pltpu.VMEM((span, local), BF16),
            pltpu.VMEM((keys, local), BF16),
            pltpu.VMEM((keys, local), BF16),
            pltpu.VMEM((span, TILE), BF16),
            pltpu.VMEM((keys, TILE), BF16),
            pltpu.VMEM((span, TILE), BF16),
            pltpu.VMEM((blocks * 16, TILE), BF16),
            pltpu.VMEM((blocks * 16, TILE), BF16),
            pltpu.VMEM((span, TILE), BF16),
            pltpu.VMEM((span, local), BF16),
            pltpu.VMEM((span, local), BF16),
            pltpu.VMEM((blocks, TILE, TILE), F32),
            pltpu.VMEM((span, local), BF16),
            pltpu.VMEM((blocks, TILE, TILE), F32),
            pltpu.VMEM((span, local), F32),
            pltpu.VMEM((span, local), F32),
            pltpu.VMEM((span, local), F32),
            pltpu.VMEM((blocks, TILE, share), BF16),
            pltpu.VMEM((blocks, TILE, share), BF16),
            pltpu.VMEM((span, share), F32),
            dma((8,)),
            dma((DIRECT,)),
            dma((relays,)),
            dma((chunks,)),
            dma((4 * PIECES,)),
            dma((2 * PIECES,)),
            dma((blocks,)),
            dma((blocks,)),
            dma((1,)),
            dma((1,)),
            dma((blocks,)),
            dma((blocks,)),
            dma((blocks,)),
            dma((blocks,)),
            dma((blocks,)),
            dma((blocks,)),
        ],
        compiler_params=pltpu.CompilerParams(
            collective_id=0, has_side_effects=True, vmem_limit_bytes=60 * 1024 * 1024
        ),
        name="layer",
    )(
        tokens,
        query_weight,
        key_weight,
        value_weight,
        out_weight,
        block_mask[0],
        frame_level,
        modulation,
    )


def solution(mesh):
    placed = (
        P(("batch", "frame"), None),
        P(None, "head"),
        P(None, "head"),
        P(None, "head"),
        P("head", None),
        P(("batch", "frame"), None, None),
        P(("batch", "frame")),
        P(),
    )
    return jax.shard_map(
        shards, mesh=mesh, in_specs=placed, out_specs=P(("batch", "frame"), "head"), check_vma=False
    )
```

```python
import functools
import math

import jax
import jax.numpy as jnp
from jax import lax
from jax.experimental import pallas as pl
from jax.experimental.pallas import tpu as pltpu
from jax.sharding import PartitionSpec as P

HEAD_DIM = 128
FRAME_TOK = 128
SINK = 128
TILE = 128
CHUNK = 32
DIRECT = 9
EARLY = 4
AHEAD = 3
BATCH = 2 * CHUNK
PIECES = 2
BLOCKED = -1e30
MESH = pl.DeviceIdType.MESH
BF16, F32 = jnp.bfloat16, jnp.float32


def layer_kernel(
    frames,
    tok_hbm,
    wq_hbm,
    wk_hbm,
    wv_hbm,
    wo_hbm,
    mask_ref,
    level_ref,
    table_hbm,
    done,
    table_ref,
    tok,
    resid,
    wq,
    wk,
    wv,
    wo_mine,
    wo_theirs,
    own,
    near,
    sink,
    qbuf,
    kbuf,
    vbuf,
    qmark,
    kmark,
    ones,
    far_rule,
    their_rule,
    their_mark,
    their_q,
    their_out,
    their_lse,
    far_out,
    far_lse,
    peak_buf,
    total_buf,
    mixed_buf,
    outgoing,
    incoming,
    kept,
    load_sem,
    send_near,
    send_x,
    recv_near,
    send_sink,
    recv_sink,
    send_q,
    recv_q,
    send_rule,
    recv_rule,
    send_o,
    recv_o,
    send_l,
    recv_l,
    send_out,
    recv_out,
):
    c = lax.axis_index("frame")
    h = lax.axis_index("head")
    span, width = own.shape
    local = wq.shape[1]
    share = done.shape[1]
    heads = local // HEAD_DIM
    blocks = span // TILE
    chunks = span // CHUNK
    relays = chunks - DIRECT
    half_rows = span // 2
    half_blocks = blocks // 2
    first_at, sink_at, last_at = span, span + half_rows, span + half_rows + SINK
    keys_end = kbuf.shape[0]

    has_near, gives_near = c >= 1, c + 1 < frames
    has_far, serves = c >= 2, c + 2 < frames
    odd, even = c % 2 == 1, c % 2 == 0

    def load(src, dst, i):
        return pltpu.make_async_copy(src, dst, load_sem.at[i])

    my_cols = pl.ds(pl.multiple_of(h * share, share), share)
    their_cols = pl.ds(pl.multiple_of((1 - h) * share, share), share)
    loads = [
        load(tok_hbm, tok, 0),
        load(wq_hbm, wq, 1),
        load(wk_hbm, wk, 2),
        load(wv_hbm, wv, 3),
        load(wo_hbm.at[:, their_cols], wo_theirs, 4),
        load(wo_hbm.at[:, my_cols], wo_mine, 5),
        load(tok_hbm.at[:, my_cols], resid, 6),
        load(table_hbm, table_ref, 7),
    ]
    for i in (0, 7, 1, 2, 3, 4, 5, 6):
        loads[i].start()

    barrier = pltpu.get_barrier_semaphore()
    pl.semaphore_signal(barrier, inc=1, device_id={"head": 1 - h}, device_id_type=MESH)
    expected = 1
    for step in (1, 2):
        for there, valid in ((c - step, c >= step), (c + step, c + step < frames)):

            @pl.when(valid)
            def _():
                pl.semaphore_signal(
                    barrier, inc=1, device_id={"frame": there}, device_id_type=MESH
                )

            expected = expected + jnp.where(valid, 1, 0)

    def rule_rows(j, valid, count):
        lane = lax.broadcasted_iota(jnp.int32, (count, TILE), 1)
        row = jnp.zeros((count, TILE), F32)
        for i in range(blocks):
            seen = mask_ref[i, j]
            if valid is not None:
                seen = seen * jnp.where(valid, 1, 0)
            row = jnp.where(lane == i, jnp.where(seen > 0, 0.0, BLOCKED), row)
        return row.astype(BF16)

    lane_at = lax.broadcasted_iota(jnp.int32, (TILE, TILE), 1)
    for i in range(blocks):
        qmark[i * TILE : (i + 1) * TILE, :] = jnp.where(lane_at == i, 1.0, 0.0).astype(BF16)
    near_tile, own_tile = (SINK + span) // TILE, (SINK + 2 * span) // TILE
    split = TILE + BATCH
    segments = [(own_tile + j, TILE, None) for j in range(blocks)]
    segments += [(near_tile, TILE, has_near), (near_tile + 1, BATCH, has_near)]
    segments += [(near_tile + 3, BATCH, has_near), (0, TILE, None)]
    segments += [(near_tile + 1, BATCH, has_near), (near_tile + 3, BATCH, has_near)]
    segments += [(near_tile + 2, TILE, has_near)]
    at = 0
    for j, count, valid in segments:
        kmark[at : at + count, :] = rule_rows(j, valid, count)
        at += count
    for j in range(blocks):
        far_rule[j * 16 : (j + 1) * 16, :] = rule_rows(SINK // TILE + j, None, 16)
    ones[...] = jnp.ones(ones.shape, BF16)

    pl.semaphore_wait(barrier, expected)

    def remote(src, dst, send, recv, device):
        return pltpu.make_async_remote_copy(
            src_ref=src,
            dst_ref=dst,
            send_sem=send,
            recv_sem=recv,
            device_id=device,
            device_id_type=MESH,
        )

    def place_of(half, k):
        if isinstance(k, int):
            low, high = (k, k + 2) if k < 2 else (k + 2, chunks + 1 - k)
            return jnp.where(half == 0, low, high)
        return jnp.where(
            half == 0, jnp.where(k < 2, k, k + 2), jnp.where(k < 2, k + 2, chunks + 1 - k)
        )

    def place(k):
        return place_of(h, k)

    def other_place(k):
        return place_of(1 - h, k)

    def chunk_rows(i):
        return pl.ds(pl.multiple_of(i * CHUNK, CHUNK), CHUNK)

    def near_copy(k):
        at = chunk_rows(place(k))
        return remote(
            own.at[at], near.at[at], send_near.at[k], recv_near.at[place(k)], {"frame": c + 1}
        )

    def x_copy(k):
        at = chunk_rows(place(k))
        return remote(
            near.at[at], near.at[at], send_x.at[k], recv_near.at[place(k)], {"head": 1 - h}
        )

    def x_arrival(k):
        at = chunk_rows(other_place(k))
        return remote(
            near.at[at], near.at[at], send_x.at[k], recv_near.at[other_place(k)], {"head": 1 - h}
        )

    def sink_place(p):
        return place(p) if p < PIECES else other_place(p - PIECES)

    def sink_z(p):
        i = sink_place(p)
        at = chunk_rows(i)
        return remote(sink.at[at], sink.at[at], send_sink.at[p], recv_sink.at[i], {"frame": c + 2})

    def sink_y(p):
        at = chunk_rows(place(p))
        return remote(
            sink.at[at],
            sink.at[at],
            send_sink.at[3 * PIECES + p],
            recv_sink.at[place(p)],
            {"frame": c + 1},
        )

    def sink_x(p, half):
        at = chunk_rows(place_of(half, p))
        return remote(
            sink.at[at],
            sink.at[at],
            send_sink.at[2 * PIECES + p],
            recv_sink.at[place_of(half, p)],
            {"head": 1 - h},
        )

    def block_rows(b):
        return pl.ds(pl.multiple_of(b * TILE, TILE), TILE)

    def q_copy(b):
        at = block_rows(b)
        return remote(qbuf.at[at], their_q.at[at], send_q.at[b], recv_q.at[b], {"frame": c - 2})

    def rule_copy():
        return remote(far_rule, their_rule, send_rule.at[0], recv_rule.at[0], {"frame": c - 2})

    def o_copy(b):
        at = block_rows(b)
        return remote(their_out.at[at], far_out.at[at], send_o.at[b], recv_o.at[b], {"frame": c + 2})

    def l_copy(b):
        return remote(
            their_lse.at[b, pl.ds(0, 8)],
            far_lse.at[b, pl.ds(0, 8)],
            send_l.at[b],
            recv_l.at[b],
            {"frame": c + 2},
        )

    def out_copy(b):
        return remote(outgoing.at[b], incoming.at[b], send_out.at[b], recv_out.at[b], {"head": 1 - h})

    def modulate(start, count):
        x = tok[pl.ds(start, count), :].astype(F32)
        mean_square = jnp.mean(x * x, axis=-1, keepdims=True)
        normed = x * lax.rsqrt(mean_square + 1e-06)
        scale_shift = table_ref[level_ref[start // FRAME_TOK]]
        return (normed * (1.0 + scale_shift[0:1]) + scale_shift[1:2]).astype(BF16)

    def batch_at(m):
        middle = (m >= 1) & (m <= chunks // 2 - 2)
        low = jnp.where(m == 0, 0, jnp.where(middle, m + 1, 1))
        high = jnp.where(m == 0, 1, jnp.where(middle, chunks // 2 - m, 0))
        return pl.multiple_of(jnp.where(h == 0, low, high) * BATCH, BATCH)

    def send_near_chunk(k, when):
        if k < DIRECT:

            @pl.when(gives_near & when)
            def _():
                near_copy(k).start()

    loads[0].wait()
    loads[7].wait()
    for m in range(AHEAD // 2):
        start = batch_at(m)
        own[pl.ds(start, BATCH), :] = modulate(start, BATCH)
        if m == 0:

            @pl.when(c == 0)
            def _():
                sink[pl.ds(start, BATCH), :] = own[pl.ds(start, BATCH), :]

            @pl.when((c == 0) & serves)
            def _():
                for p in range(PIECES):
                    sink_z(p).start()

        send_near_chunk(2 * m, c >= 0)
        send_near_chunk(2 * m + 1, c >= 0)

    @pl.when(c == 0)
    def _():
        start = pl.multiple_of((1 - h) * BATCH, BATCH)
        sink[pl.ds(start, BATCH), :] = modulate(start, BATCH)

        @pl.when(serves)
        def _():
            for p in range(PIECES, 2 * PIECES):
                sink_z(p).start()

    def rest(m, carry):
        start = batch_at(m)
        own[pl.ds(start, BATCH), :] = modulate(start, BATCH)
        return carry

    lax.fori_loop(AHEAD // 2, chunks // 2, rest, 0)
    send_near_chunk(2, even)
    for k in range(2, DIRECT):
        send_near_chunk(k, odd)

    def project(flat, weight, dst, start, scale=None):
        res = jnp.dot(flat, weight[...], preferred_element_type=F32)
        if scale is not None:
            res = res * scale
        dst[start : start + flat.shape[0], :] = res.astype(BF16)

    def near_point(k):
        @pl.when(has_near)
        def _():
            near_copy(k).wait_recv()
            if k < relays:
                x_copy(k).start()

        send_near_chunk(k + AHEAD, even)

    def sink_even(p, lo, hi):
        @pl.when(even & (c >= 2 * lo) & (c < 2 * hi))
        def _():
            sink_z(p).wait_recv()

            @pl.when(serves)
            def _():
                sink_z(p).start()

            if p < PIECES:
                sink_y(p).start()

    def sink_odd(p, lo, hi):
        @pl.when(odd & (c >= 2 * lo) & (c < 2 * hi))
        def _():
            sink_y(p).wait_recv()
            sink_x(p, h).start()

    def head_cols(n):
        return slice(n * HEAD_DIM, (n + 1) * HEAD_DIM)

    def score(q_ref, q_at, q_stop, k_at, k_stop, mark, mark_at, n):
        left = jnp.concatenate([q_ref[q_at:q_stop, head_cols(n)], qmark[q_at:q_stop, :]], axis=1)
        marks = mark[mark_at : mark_at + k_stop - k_at, :]
        right = jnp.concatenate([kbuf[k_at:k_stop, head_cols(n)], marks], axis=1)
        return lax.dot_general(left, right, (((1,), (1,)), ((), ())), preferred_element_type=F32)

    def mix(num, k_at, k_stop, n):
        right = jnp.concatenate(
            [vbuf[k_at:k_stop, head_cols(n)], ones[0 : k_stop - k_at, :]], axis=1
        )
        both = jnp.dot(num.astype(BF16), right, preferred_element_type=F32)
        return both[:, :HEAD_DIM], both[:, HEAD_DIM:]

    def wide(column, shape):
        return jnp.broadcast_to(column, shape)

    loads[1].wait()
    project(own[...], wq, qbuf, 0, 1.0 / math.sqrt(HEAD_DIM))

    @pl.when(has_far)
    def _():
        rule_copy().start()
        for b in range(blocks):
            q_copy(b).start()

    near_point(0)
    sink_even(0, 1, 2)
    loads[2].wait()
    project(own[...], wk, kbuf, 0)
    loads[3].wait()
    project(own[...], wv, vbuf, 0)

    def own_heads(lo, hi):
        for n in range(lo, hi):
            scores = score(qbuf, 0, span, 0, span, kmark, 0, n)
            peak = jnp.max(scores, axis=-1, keepdims=True)
            rows_out, total = mix(jnp.exp(scores - peak), 0, span, n)
            peak_buf[:, head_cols(n)] = wide(peak, total.shape)
            total_buf[:, head_cols(n)] = total
            mixed_buf[:, head_cols(n)] = rows_out

    sink_even(1, 1, 2)
    own_heads(0, heads // 2)
    near_point(1)
    sink_even(2, 1, 2)
    sink_even(0, 2, 3)
    own_heads(heads // 2, heads)
    near_point(2)
    sink_even(3, 1, 2)
    sink_even(1, 2, 3)
    sink_odd(0, 1, 2)
    sink_even(0, 3, frames)
    near_point(3)
    sink_even(2, 2, 3)
    sink_even(1, 3, frames)
    sink_odd(1, 1, 2)

    def serve(g):
        lo, hi = g * half_rows, (g + 1) * half_rows

        @pl.when(serves)
        def _():
            if g == 0:
                rule_copy().wait_recv()
                for j in range(blocks):
                    small = their_rule[j * 16 : (j + 1) * 16, :]
                    their_mark[j * TILE : (j + 1) * TILE, :] = jnp.concatenate(
                        [small] * (TILE // 16), axis=0
                    )
            for b in range(g * half_blocks, (g + 1) * half_blocks):
                q_copy(b).wait_recv()
            lanes = lax.broadcasted_iota(jnp.int32, (half_rows, HEAD_DIM), 1)
            lse_all = jnp.zeros((half_rows, HEAD_DIM), F32)
            for n in range(heads):
                scores = score(their_q, lo, hi, 0, span, their_mark, 0, n)
                peak = jnp.max(scores, axis=-1, keepdims=True)
                rows_out, total = mix(jnp.exp(scores - peak), 0, span, n)
                their_out[lo:hi, head_cols(n)] = (rows_out / total).astype(BF16)
                lse_all = jnp.where(lanes == n, peak + jnp.log(total), lse_all)
            for b in range(half_blocks):
                their_lse[g * half_blocks + b] = lse_all[b * TILE : (b + 1) * TILE, :].T
            for b in range(g * half_blocks, (g + 1) * half_blocks):
                l_copy(b).start()
                o_copy(b).start()

    near_point(4)
    sink_even(3, 2, 3)
    sink_odd(0, 2, 3)

    @pl.when(has_near)
    def _():
        for k in range(EARLY):
            x_arrival(k).wait_recv()
        flat = jnp.concatenate([near[0:split, :], near[span - BATCH : span, :]], axis=0)
        project(flat, wk, kbuf, first_at)
        project(flat, wv, vbuf, first_at)

    @pl.when(jnp.logical_not(has_near))
    def _():
        for buf in (kbuf, vbuf):
            buf[first_at:sink_at, :] = jnp.zeros((half_rows, local), BF16)
            buf[last_at:keys_end, :] = jnp.zeros((half_rows, local), BF16)

    near_point(5)
    sink_even(2, 3, frames)
    sink_odd(1, 2, 3)
    sink_odd(0, 3, frames)
    near_point(6)
    sink_even(3, 3, frames)
    sink_odd(1, 3, frames)
    serve(0)

    def project_sink():
        project(sink[...], wk, kbuf, sink_at)
        project(sink[...], wv, vbuf, sink_at)

    for n in range(heads):
        scores = score(qbuf, 0, span, first_at, sink_at, kmark, first_at, n)
        before = peak_buf[:, head_cols(n)]
        peak = jnp.maximum(jnp.max(scores, axis=-1, keepdims=True), before)
        keep = jnp.exp(before - peak)
        spread = jnp.concatenate([peak] * (scores.shape[1] // HEAD_DIM), axis=1)
        rows_out, total = mix(jnp.exp(scores - spread), first_at, sink_at, n)
        peak_buf[:, head_cols(n)] = peak
        total_buf[:, head_cols(n)] = total_buf[:, head_cols(n)] * keep + total
        mixed_buf[:, head_cols(n)] = mixed_buf[:, head_cols(n)] * keep + rows_out

    for i in (4, 5, 6):
        loads[i].wait()

    tail_at = keys_end - TILE

    @pl.when(has_near)
    def _():
        for k in range(EARLY, EARLY + 2):
            x_arrival(k).wait_recv()
        flat = jnp.concatenate(
            [near[split : split + BATCH, :], near[span - 2 * BATCH : span - BATCH, :]], axis=0
        )
        project(flat, wk, kbuf, last_at)
        project(flat, wv, vbuf, last_at)

    @pl.when(has_far & odd)
    def _():
        for p in range(PIECES):
            sink_x(p, 1 - h).wait_recv()

    @pl.when(c == 1)
    def _():
        sink[...] = near[0:SINK, :]

    project_sink()

    @pl.when(has_near)
    def _():
        for k in range(relays, DIRECT):
            near_copy(k).wait_recv()
        for k in range(EARLY + 2, relays):
            x_arrival(k).wait_recv()
        flat = near[split + BATCH : span - 2 * BATCH, :]
        project(flat, wk, kbuf, tail_at)
        project(flat, wv, vbuf, tail_at)

    @pl.when(jnp.logical_not(has_far))
    def _():
        far_out[...] = jnp.zeros(far_out.shape, BF16)
        far_lse[...] = jnp.full(far_lse.shape, BLOCKED, F32)

    def last_keys(g):
        lo, hi = g * half_rows, (g + 1) * half_rows
        for n in range(heads):
            scores = score(qbuf, lo, hi, sink_at, keys_end, kmark, sink_at, n)
            before = peak_buf[lo:hi, head_cols(n)]
            peak = jnp.maximum(jnp.max(scores, axis=-1, keepdims=True), before)
            keep = jnp.exp(before - peak)
            spread = jnp.concatenate([peak] * (scores.shape[1] // HEAD_DIM), axis=1)
            rows_out, total = mix(jnp.exp(scores - spread), sink_at, keys_end, n)
            peak_buf[lo:hi, head_cols(n)] = peak
            total_buf[lo:hi, head_cols(n)] = total_buf[lo:hi, head_cols(n)] * keep + total
            mixed_buf[lo:hi, head_cols(n)] = mixed_buf[lo:hi, head_cols(n)] * keep + rows_out

    def send_block(b):
        lo, hi = b * TILE, (b + 1) * TILE

        @pl.when(has_far)
        def _():
            l_copy(b).wait_recv()
            o_copy(b).wait_recv()

        far_cols = far_lse[b].T
        parts = []
        for n in range(heads):
            before = peak_buf[lo:hi, head_cols(n)]
            far_peak = wide(far_cols[:, n : n + 1], before.shape)
            peak = jnp.maximum(before, far_peak)
            keep = jnp.exp(before - peak)
            far_weight = jnp.exp(far_peak - peak)
            total = total_buf[lo:hi, head_cols(n)] * keep + far_weight
            rows_out = (
                mixed_buf[lo:hi, head_cols(n)] * keep
                + far_out[lo:hi, head_cols(n)].astype(F32) * far_weight
            )
            parts.append((rows_out / total).astype(BF16))
        attended = jnp.concatenate(parts, axis=1)
        outgoing[b] = jnp.dot(attended, wo_theirs[...], preferred_element_type=F32).astype(BF16)
        out_copy(b).start()
        return attended

    def keep_block(b, attended):
        lo, hi = b * TILE, (b + 1) * TILE
        kept[lo:hi, :] = resid[lo:hi, :].astype(F32) + jnp.dot(
            attended, wo_mine[...], preferred_element_type=F32
        )

    last_keys(0)
    first = send_block(0)
    serve(1)
    second = send_block(1)
    keep_block(0, first)
    last_keys(1)
    keep_block(1, second)
    for b in range(half_blocks, blocks):
        keep_block(b, send_block(b))

    for b in range(blocks):
        at = slice(b * TILE, (b + 1) * TILE)
        out_copy(b).wait_recv()
        done[at, :] = (kept[at, :] + incoming[b].astype(F32)).astype(BF16)

    for b in range(blocks):
        out_copy(b).wait_send()

    @pl.when(gives_near)
    def _():
        for k in range(DIRECT):
            near_copy(k).wait_send()

    @pl.when(has_near)
    def _():
        for k in range(relays):
            x_copy(k).wait_send()

    @pl.when(serves & even)
    def _():
        for p in range(2 * PIECES):
            sink_z(p).wait_send()

    @pl.when(serves)
    def _():
        for b in range(blocks):
            o_copy(b).wait_send()
            l_copy(b).wait_send()

    @pl.when(has_far & odd)
    def _():
        for p in range(PIECES):
            sink_x(p, h).wait_send()

    @pl.when(has_far & even)
    def _():
        for p in range(PIECES):
            sink_y(p).wait_send()

    @pl.when(has_far)
    def _():
        rule_copy().wait_send()
        for b in range(blocks):
            q_copy(b).wait_send()


def shards(
    tokens, query_weight, key_weight, value_weight, out_weight, block_mask, frame_level, modulation
):
    span, width = tokens.shape
    local = query_weight.shape[1]
    share = width // lax.axis_size("head")
    chunks = span // CHUNK
    relays = chunks - DIRECT
    blocks = span // TILE
    keys = SINK + 2 * span
    dma = pltpu.SemaphoreType.DMA
    anywhere = pl.BlockSpec(memory_space=pl.ANY)
    smem = pl.BlockSpec(memory_space=pltpu.SMEM)
    return pl.pallas_call(
        functools.partial(layer_kernel, lax.axis_size("frame")),
        out_shape=pltpu.VMEM((span, share), BF16),
        in_specs=[anywhere] * 5 + [smem, smem, anywhere],
        out_specs=pl.BlockSpec(memory_space=pltpu.VMEM),
        scratch_shapes=[
            pltpu.VMEM(modulation.shape, F32),
            pltpu.VMEM((span, width), BF16),
            pltpu.VMEM((span, share), BF16),
            pltpu.VMEM((width, local), BF16),
            pltpu.VMEM((width, local), BF16),
            pltpu.VMEM((width, local), BF16),
            pltpu.VMEM((local, share), BF16),
            pltpu.VMEM((local, share), BF16),
            pltpu.VMEM((span, width), BF16),
            pltpu.VMEM((span, width), BF16),
            pltpu.VMEM((SINK, width), BF16),
            pltpu.VMEM((span, local), BF16),
            pltpu.VMEM((keys, local), BF16),
            pltpu.VMEM((keys, local), BF16),
            pltpu.VMEM((span, TILE), BF16),
            pltpu.VMEM((keys, TILE), BF16),
            pltpu.VMEM((span, TILE), BF16),
            pltpu.VMEM((blocks * 16, TILE), BF16),
            pltpu.VMEM((blocks * 16, TILE), BF16),
            pltpu.VMEM((span, TILE), BF16),
            pltpu.VMEM((span, local), BF16),
            pltpu.VMEM((span, local), BF16),
            pltpu.VMEM((blocks, TILE, TILE), F32),
            pltpu.VMEM((span, local), BF16),
            pltpu.VMEM((blocks, TILE, TILE), F32),
            pltpu.VMEM((span, local), F32),
            pltpu.VMEM((span, local), F32),
            pltpu.VMEM((span, local), F32),
            pltpu.VMEM((blocks, TILE, share), BF16),
            pltpu.VMEM((blocks, TILE, share), BF16),
            pltpu.VMEM((span, share), F32),
            dma((8,)),
            dma((DIRECT,)),
            dma((relays,)),
            dma((chunks,)),
            dma((4 * PIECES,)),
            dma((2 * PIECES,)),
            dma((blocks,)),
            dma((blocks,)),
            dma((1,)),
            dma((1,)),
            dma((blocks,)),
            dma((blocks,)),
            dma((blocks,)),
            dma((blocks,)),
            dma((blocks,)),
            dma((blocks,)),
        ],
        compiler_params=pltpu.CompilerParams(
            collective_id=0, has_side_effects=True, vmem_limit_bytes=60 * 1024 * 1024
        ),
        name="layer",
    )(
        tokens,
        query_weight,
        key_weight,
        value_weight,
        out_weight,
        block_mask[0],
        frame_level,
        modulation,
    )


def solution(mesh):
    placed = (
        P(("batch", "frame"), None),
        P(None, "head"),
        P(None, "head"),
        P(None, "head"),
        P("head", None),
        P(("batch", "frame"), None, None),
        P(("batch", "frame")),
        P(),
    )
    return jax.shard_map(
        shards, mesh=mesh, in_specs=placed, out_specs=P(("batch", "frame"), "head"), check_vma=False
    )
```

```python
import functools
import math

import jax
import jax.numpy as jnp
from jax import lax
from jax.experimental import pallas as pl
from jax.experimental.pallas import tpu as pltpu
from jax.sharding import PartitionSpec as P

HEAD_DIM = 128
FRAME_TOK = 128
SINK = 128
TILE = 128
CHUNK = 32
DIRECT = 9
EARLY = 4
AHEAD = 3
BATCH = 2 * CHUNK
PIECES = 2
BLOCKED = -1e30
MESH = pl.DeviceIdType.MESH
BF16, F32 = jnp.bfloat16, jnp.float32


def layer_kernel(
    frames,
    tok_hbm,
    wq_hbm,
    wk_hbm,
    wv_hbm,
    wo_hbm,
    mask_ref,
    level_ref,
    table_hbm,
    done,
    table_ref,
    tok,
    resid,
    wq,
    wk,
    wv,
    wo_mine,
    wo_theirs,
    own,
    near,
    sink,
    qbuf,
    kbuf,
    vbuf,
    qmark,
    kmark,
    ones,
    far_rule,
    their_rule,
    their_mark,
    their_q,
    their_out,
    their_lse,
    far_out,
    far_lse,
    peak_buf,
    total_buf,
    mixed_buf,
    outgoing,
    incoming,
    kept,
    load_sem,
    send_near,
    send_x,
    recv_near,
    send_sink,
    recv_sink,
    send_q,
    recv_q,
    send_rule,
    recv_rule,
    send_o,
    recv_o,
    send_l,
    recv_l,
    send_out,
    recv_out,
):
    c = lax.axis_index("frame")
    h = lax.axis_index("head")
    span, width = own.shape
    local = wq.shape[1]
    share = done.shape[1]
    heads = local // HEAD_DIM
    blocks = span // TILE
    chunks = span // CHUNK
    relays = chunks - DIRECT
    half_rows = span // 2
    half_blocks = blocks // 2
    first_at, sink_at, last_at = span, span + half_rows, span + half_rows + SINK
    keys_end = kbuf.shape[0]

    has_near, gives_near = c >= 1, c + 1 < frames
    has_far, serves = c >= 2, c + 2 < frames
    odd, even = c % 2 == 1, c % 2 == 0

    barrier = pltpu.get_barrier_semaphore()
    pl.semaphore_signal(barrier, inc=1, device_id={"head": 1 - h}, device_id_type=MESH)
    expected = 1
    for step in (1, 2):
        for there, valid in ((c - step, c >= step), (c + step, c + step < frames)):

            @pl.when(valid)
            def _():
                pl.semaphore_signal(
                    barrier, inc=1, device_id={"frame": there}, device_id_type=MESH
                )

            expected = expected + jnp.where(valid, 1, 0)

    def load(src, dst, i):
        return pltpu.make_async_copy(src, dst, load_sem.at[i])

    my_cols = pl.ds(pl.multiple_of(h * share, share), share)
    their_cols = pl.ds(pl.multiple_of((1 - h) * share, share), share)
    loads = [
        load(tok_hbm, tok, 0),
        load(wq_hbm, wq, 1),
        load(wk_hbm, wk, 2),
        load(wv_hbm, wv, 3),
        load(wo_hbm.at[:, their_cols], wo_theirs, 4),
        load(wo_hbm.at[:, my_cols], wo_mine, 5),
        load(tok_hbm.at[:, my_cols], resid, 6),
        load(table_hbm, table_ref, 7),
    ]
    for i in (0, 7, 1, 2, 3, 4, 5, 6):
        loads[i].start()

    def rule_rows(j, valid, count):
        lane = lax.broadcasted_iota(jnp.int32, (count, TILE), 1)
        row = jnp.zeros((count, TILE), F32)
        for i in range(blocks):
            seen = mask_ref[i, j]
            if valid is not None:
                seen = seen * jnp.where(valid, 1, 0)
            row = jnp.where(lane == i, jnp.where(seen > 0, 0.0, BLOCKED), row)
        return row.astype(BF16)

    lane_at = lax.broadcasted_iota(jnp.int32, (TILE, TILE), 1)
    for i in range(blocks):
        qmark[i * TILE : (i + 1) * TILE, :] = jnp.where(lane_at == i, 1.0, 0.0).astype(BF16)
    near_tile, own_tile = (SINK + span) // TILE, (SINK + 2 * span) // TILE
    split = TILE + BATCH
    segments = [(own_tile + j, TILE, None) for j in range(blocks)]
    segments += [(near_tile, TILE, has_near), (near_tile + 1, BATCH, has_near)]
    segments += [(near_tile + 3, BATCH, has_near), (0, TILE, None)]
    segments += [(near_tile + 1, BATCH, has_near), (near_tile + 3, BATCH, has_near)]
    segments += [(near_tile + 2, TILE, has_near)]
    at = 0
    for j, count, valid in segments:
        kmark[at : at + count, :] = rule_rows(j, valid, count)
        at += count
    for j in range(blocks):
        far_rule[j * 16 : (j + 1) * 16, :] = rule_rows(SINK // TILE + j, None, 16)
    ones[...] = jnp.ones(ones.shape, BF16)

    pl.semaphore_wait(barrier, expected)

    def remote(src, dst, send, recv, device):
        return pltpu.make_async_remote_copy(
            src_ref=src,
            dst_ref=dst,
            send_sem=send,
            recv_sem=recv,
            device_id=device,
            device_id_type=MESH,
        )

    def place_of(half, k):
        if isinstance(k, int):
            low, high = (k, k + 2) if k < 2 else (k + 2, chunks + 1 - k)
            return jnp.where(half == 0, low, high)
        return jnp.where(
            half == 0, jnp.where(k < 2, k, k + 2), jnp.where(k < 2, k + 2, chunks + 1 - k)
        )

    def place(k):
        return place_of(h, k)

    def other_place(k):
        return place_of(1 - h, k)

    def chunk_rows(i):
        return pl.ds(pl.multiple_of(i * CHUNK, CHUNK), CHUNK)

    def near_copy(k):
        at = chunk_rows(place(k))
        return remote(
            own.at[at], near.at[at], send_near.at[k], recv_near.at[place(k)], {"frame": c + 1}
        )

    def x_copy(k):
        at = chunk_rows(place(k))
        return remote(
            near.at[at], near.at[at], send_x.at[k], recv_near.at[place(k)], {"head": 1 - h}
        )

    def x_arrival(k):
        at = chunk_rows(other_place(k))
        return remote(
            near.at[at], near.at[at], send_x.at[k], recv_near.at[other_place(k)], {"head": 1 - h}
        )

    def sink_place(p):
        return place(p) if p < PIECES else other_place(p - PIECES)

    def sink_z(p):
        i = sink_place(p)
        at = chunk_rows(i)
        return remote(sink.at[at], sink.at[at], send_sink.at[p], recv_sink.at[i], {"frame": c + 2})

    def sink_y(p):
        at = chunk_rows(place(p))
        return remote(
            sink.at[at],
            sink.at[at],
            send_sink.at[3 * PIECES + p],
            recv_sink.at[place(p)],
            {"frame": c + 1},
        )

    def sink_x(p, half):
        at = chunk_rows(place_of(half, p))
        return remote(
            sink.at[at],
            sink.at[at],
            send_sink.at[2 * PIECES + p],
            recv_sink.at[place_of(half, p)],
            {"head": 1 - h},
        )

    def block_rows(b):
        return pl.ds(pl.multiple_of(b * TILE, TILE), TILE)

    def q_copy(b):
        at = block_rows(b)
        return remote(qbuf.at[at], their_q.at[at], send_q.at[b], recv_q.at[b], {"frame": c - 2})

    def rule_copy():
        return remote(far_rule, their_rule, send_rule.at[0], recv_rule.at[0], {"frame": c - 2})

    def o_copy(b):
        at = block_rows(b)
        return remote(their_out.at[at], far_out.at[at], send_o.at[b], recv_o.at[b], {"frame": c + 2})

    def l_copy(b):
        return remote(
            their_lse.at[b, pl.ds(0, 8)],
            far_lse.at[b, pl.ds(0, 8)],
            send_l.at[b],
            recv_l.at[b],
            {"frame": c + 2},
        )

    def out_copy(b):
        return remote(outgoing.at[b], incoming.at[b], send_out.at[b], recv_out.at[b], {"head": 1 - h})

    def modulate(start, count):
        x = tok[pl.ds(start, count), :].astype(F32)
        mean_square = jnp.mean(x * x, axis=-1, keepdims=True)
        normed = x * lax.rsqrt(mean_square + 1e-06)
        scale_shift = table_ref[level_ref[start // FRAME_TOK]]
        return (normed * (1.0 + scale_shift[0:1]) + scale_shift[1:2]).astype(BF16)

    def batch_at(m):
        middle = (m >= 1) & (m <= chunks // 2 - 2)
        low = jnp.where(m == 0, 0, jnp.where(middle, m + 1, 1))
        high = jnp.where(m == 0, 1, jnp.where(middle, chunks // 2 - m, 0))
        return pl.multiple_of(jnp.where(h == 0, low, high) * BATCH, BATCH)

    def send_near_chunk(k, when):
        if k < DIRECT:

            @pl.when(gives_near & when)
            def _():
                near_copy(k).start()

    loads[0].wait()
    loads[7].wait()
    for m in range(AHEAD // 2):
        start = batch_at(m)
        own[pl.ds(start, BATCH), :] = modulate(start, BATCH)
        if m == 0:

            @pl.when(c == 0)
            def _():
                sink[pl.ds(start, BATCH), :] = own[pl.ds(start, BATCH), :]

            @pl.when((c == 0) & serves)
            def _():
                for p in range(PIECES):
                    sink_z(p).start()

        send_near_chunk(2 * m, c >= 0)
        send_near_chunk(2 * m + 1, c >= 0)

    @pl.when(c == 0)
    def _():
        start = pl.multiple_of((1 - h) * BATCH, BATCH)
        sink[pl.ds(start, BATCH), :] = modulate(start, BATCH)

        @pl.when(serves)
        def _():
            for p in range(PIECES, 2 * PIECES):
                sink_z(p).start()

    def rest(m, carry):
        start = batch_at(m)
        own[pl.ds(start, BATCH), :] = modulate(start, BATCH)
        return carry

    lax.fori_loop(AHEAD // 2, chunks // 2, rest, 0)
    send_near_chunk(2, even)
    for k in range(2, DIRECT):
        send_near_chunk(k, odd)

    def project(flat, weight, dst, start, scale=None):
        res = jnp.dot(flat, weight[...], preferred_element_type=F32)
        if scale is not None:
            res = res * scale
        dst[start : start + flat.shape[0], :] = res.astype(BF16)

    def near_point(k):
        @pl.when(has_near)
        def _():
            near_copy(k).wait_recv()
            if k < relays:
                x_copy(k).start()

        send_near_chunk(k + AHEAD, even)

    def sink_even(p, lo, hi):
        @pl.when(even & (c >= 2 * lo) & (c < 2 * hi))
        def _():
            sink_z(p).wait_recv()

            @pl.when(serves)
            def _():
                sink_z(p).start()

            if p < PIECES:
                sink_y(p).start()

    def sink_odd(p, lo, hi):
        @pl.when(odd & (c >= 2 * lo) & (c < 2 * hi))
        def _():
            sink_y(p).wait_recv()
            sink_x(p, h).start()

    def head_cols(n):
        return slice(n * HEAD_DIM, (n + 1) * HEAD_DIM)

    def score(q_ref, q_at, q_stop, k_at, k_stop, mark, mark_at, n):
        left = jnp.concatenate([q_ref[q_at:q_stop, head_cols(n)], qmark[q_at:q_stop, :]], axis=1)
        marks = mark[mark_at : mark_at + k_stop - k_at, :]
        right = jnp.concatenate([kbuf[k_at:k_stop, head_cols(n)], marks], axis=1)
        return lax.dot_general(left, right, (((1,), (1,)), ((), ())), preferred_element_type=F32)

    def mix(num, k_at, k_stop, n):
        right = jnp.concatenate(
            [vbuf[k_at:k_stop, head_cols(n)], ones[0 : k_stop - k_at, :]], axis=1
        )
        both = jnp.dot(num.astype(BF16), right, preferred_element_type=F32)
        return both[:, :HEAD_DIM], both[:, HEAD_DIM:]

    def wide(column, shape):
        return jnp.broadcast_to(column, shape)

    loads[1].wait()
    project(own[...], wq, qbuf, 0, 1.0 / math.sqrt(HEAD_DIM))

    @pl.when(has_far)
    def _():
        rule_copy().start()
        for b in range(blocks):
            q_copy(b).start()

    near_point(0)
    sink_even(0, 1, 2)
    loads[2].wait()
    project(own[...], wk, kbuf, 0)
    loads[3].wait()
    project(own[...], wv, vbuf, 0)

    def own_heads(lo, hi):
        for n in range(lo, hi):
            scores = score(qbuf, 0, span, 0, span, kmark, 0, n)
            peak = jnp.max(scores, axis=-1, keepdims=True)
            rows_out, total = mix(jnp.exp(scores - peak), 0, span, n)
            peak_buf[:, head_cols(n)] = wide(peak, total.shape)
            total_buf[:, head_cols(n)] = total
            mixed_buf[:, head_cols(n)] = rows_out

    sink_even(1, 1, 2)
    own_heads(0, heads // 2)
    near_point(1)
    sink_even(2, 1, 2)
    sink_even(0, 2, 3)
    own_heads(heads // 2, heads)
    near_point(2)
    sink_even(3, 1, 2)
    sink_even(1, 2, 3)
    sink_odd(0, 1, 2)
    sink_even(0, 3, frames)
    near_point(3)
    sink_even(2, 2, 3)
    sink_even(1, 3, frames)
    sink_odd(1, 1, 2)

    def serve(g):
        lo, hi = g * half_rows, (g + 1) * half_rows

        @pl.when(serves)
        def _():
            if g == 0:
                rule_copy().wait_recv()
                for j in range(blocks):
                    small = their_rule[j * 16 : (j + 1) * 16, :]
                    their_mark[j * TILE : (j + 1) * TILE, :] = jnp.concatenate(
                        [small] * (TILE // 16), axis=0
                    )
            for b in range(g * half_blocks, (g + 1) * half_blocks):
                q_copy(b).wait_recv()
            lanes = lax.broadcasted_iota(jnp.int32, (half_rows, HEAD_DIM), 1)
            lse_all = jnp.zeros((half_rows, HEAD_DIM), F32)
            for n in range(heads):
                scores = score(their_q, lo, hi, 0, span, their_mark, 0, n)
                peak = jnp.max(scores, axis=-1, keepdims=True)
                rows_out, total = mix(jnp.exp(scores - peak), 0, span, n)
                their_out[lo:hi, head_cols(n)] = (rows_out / total).astype(BF16)
                lse_all = jnp.where(lanes == n, peak + jnp.log(total), lse_all)
            for b in range(half_blocks):
                their_lse[g * half_blocks + b] = lse_all[b * TILE : (b + 1) * TILE, :].T
            for b in range(g * half_blocks, (g + 1) * half_blocks):
                l_copy(b).start()
                o_copy(b).start()

    sink_odd(0, 2, 3)
    near_point(4)
    sink_even(3, 2, 3)

    @pl.when(has_near)
    def _():
        for k in range(EARLY):
            x_arrival(k).wait_recv()
        flat = jnp.concatenate([near[0:split, :], near[span - BATCH : span, :]], axis=0)
        project(flat, wk, kbuf, first_at)
        project(flat, wv, vbuf, first_at)

    @pl.when(jnp.logical_not(has_near))
    def _():
        for buf in (kbuf, vbuf):
            buf[first_at:sink_at, :] = jnp.zeros((half_rows, local), BF16)
            buf[last_at:keys_end, :] = jnp.zeros((half_rows, local), BF16)

    sink_odd(1, 2, 3)
    near_point(5)
    sink_even(2, 3, frames)
    sink_odd(0, 3, frames)
    near_point(6)
    sink_even(3, 3, frames)
    sink_odd(1, 3, frames)
    serve(0)

    def project_sink():
        project(sink[...], wk, kbuf, sink_at)
        project(sink[...], wv, vbuf, sink_at)

    for n in range(heads):
        scores = score(qbuf, 0, span, first_at, sink_at, kmark, first_at, n)
        before = peak_buf[:, head_cols(n)]
        peak = jnp.maximum(jnp.max(scores, axis=-1, keepdims=True), before)
        keep = jnp.exp(before - peak)
        spread = jnp.concatenate([peak] * (scores.shape[1] // HEAD_DIM), axis=1)
        rows_out, total = mix(jnp.exp(scores - spread), first_at, sink_at, n)
        peak_buf[:, head_cols(n)] = peak
        total_buf[:, head_cols(n)] = total_buf[:, head_cols(n)] * keep + total
        mixed_buf[:, head_cols(n)] = mixed_buf[:, head_cols(n)] * keep + rows_out

    for i in (4, 5, 6):
        loads[i].wait()

    tail_at = keys_end - TILE

    @pl.when(has_near)
    def _():
        for k in range(EARLY, EARLY + 2):
            x_arrival(k).wait_recv()
        flat = jnp.concatenate(
            [near[split : split + BATCH, :], near[span - 2 * BATCH : span - BATCH, :]], axis=0
        )
        project(flat, wk, kbuf, last_at)
        project(flat, wv, vbuf, last_at)

    @pl.when(has_far & odd)
    def _():
        for p in range(PIECES):
            sink_x(p, 1 - h).wait_recv()

    @pl.when(c == 1)
    def _():
        sink[...] = near[0:SINK, :]

    project_sink()

    @pl.when(has_near)
    def _():
        for k in range(relays, DIRECT):
            near_copy(k).wait_recv()
        for k in range(EARLY + 2, relays):
            x_arrival(k).wait_recv()
        flat = near[split + BATCH : span - 2 * BATCH, :]
        project(flat, wk, kbuf, tail_at)
        project(flat, wv, vbuf, tail_at)

    @pl.when(jnp.logical_not(has_far))
    def _():
        far_out[...] = jnp.zeros(far_out.shape, BF16)
        far_lse[...] = jnp.full(far_lse.shape, BLOCKED, F32)

    def last_keys(g):
        lo, hi = g * half_rows, (g + 1) * half_rows
        for n in range(heads):
            scores = score(qbuf, lo, hi, sink_at, keys_end, kmark, sink_at, n)
            before = peak_buf[lo:hi, head_cols(n)]
            peak = jnp.maximum(jnp.max(scores, axis=-1, keepdims=True), before)
            keep = jnp.exp(before - peak)
            spread = jnp.concatenate([peak] * (scores.shape[1] // HEAD_DIM), axis=1)
            rows_out, total = mix(jnp.exp(scores - spread), sink_at, keys_end, n)
            peak_buf[lo:hi, head_cols(n)] = peak
            total_buf[lo:hi, head_cols(n)] = total_buf[lo:hi, head_cols(n)] * keep + total
            mixed_buf[lo:hi, head_cols(n)] = mixed_buf[lo:hi, head_cols(n)] * keep + rows_out

    def send_block(b):
        lo, hi = b * TILE, (b + 1) * TILE

        @pl.when(has_far)
        def _():
            l_copy(b).wait_recv()
            o_copy(b).wait_recv()

        far_cols = far_lse[b].T
        parts = []
        for n in range(heads):
            before = peak_buf[lo:hi, head_cols(n)]
            far_peak = wide(far_cols[:, n : n + 1], before.shape)
            peak = jnp.maximum(before, far_peak)
            keep = jnp.exp(before - peak)
            far_weight = jnp.exp(far_peak - peak)
            total = total_buf[lo:hi, head_cols(n)] * keep + far_weight
            rows_out = (
                mixed_buf[lo:hi, head_cols(n)] * keep
                + far_out[lo:hi, head_cols(n)].astype(F32) * far_weight
            )
            parts.append((rows_out / total).astype(BF16))
        attended = jnp.concatenate(parts, axis=1)
        outgoing[b] = jnp.dot(attended, wo_theirs[...], preferred_element_type=F32).astype(BF16)
        out_copy(b).start()
        return attended

    def keep_block(b, attended):
        lo, hi = b * TILE, (b + 1) * TILE
        kept[lo:hi, :] = resid[lo:hi, :].astype(F32) + jnp.dot(
            attended, wo_mine[...], preferred_element_type=F32
        )

    last_keys(0)
    first = send_block(0)
    serve(1)
    second = send_block(1)
    keep_block(0, first)
    last_keys(1)
    keep_block(1, second)
    for b in range(half_blocks, blocks):
        keep_block(b, send_block(b))

    for b in range(blocks):
        at = slice(b * TILE, (b + 1) * TILE)
        out_copy(b).wait_recv()
        done[at, :] = (kept[at, :] + incoming[b].astype(F32)).astype(BF16)

    for b in range(blocks):
        out_copy(b).wait_send()

    @pl.when(gives_near)
    def _():
        for k in range(DIRECT):
            near_copy(k).wait_send()

    @pl.when(has_near)
    def _():
        for k in range(relays):
            x_copy(k).wait_send()

    @pl.when(serves & even)
    def _():
        for p in range(2 * PIECES):
            sink_z(p).wait_send()

    @pl.when(serves)
    def _():
        for b in range(blocks):
            o_copy(b).wait_send()
            l_copy(b).wait_send()

    @pl.when(has_far & odd)
    def _():
        for p in range(PIECES):
            sink_x(p, h).wait_send()

    @pl.when(has_far & even)
    def _():
        for p in range(PIECES):
            sink_y(p).wait_send()

    @pl.when(has_far)
    def _():
        rule_copy().wait_send()
        for b in range(blocks):
            q_copy(b).wait_send()


def shards(
    tokens, query_weight, key_weight, value_weight, out_weight, block_mask, frame_level, modulation
):
    span, width = tokens.shape
    local = query_weight.shape[1]
    share = width // lax.axis_size("head")
    chunks = span // CHUNK
    relays = chunks - DIRECT
    blocks = span // TILE
    keys = SINK + 2 * span
    dma = pltpu.SemaphoreType.DMA
    anywhere = pl.BlockSpec(memory_space=pl.ANY)
    smem = pl.BlockSpec(memory_space=pltpu.SMEM)
    return pl.pallas_call(
        functools.partial(layer_kernel, lax.axis_size("frame")),
        out_shape=pltpu.VMEM((span, share), BF16),
        in_specs=[anywhere] * 5 + [smem, smem, anywhere],
        out_specs=pl.BlockSpec(memory_space=pltpu.VMEM),
        scratch_shapes=[
            pltpu.VMEM(modulation.shape, F32),
            pltpu.VMEM((span, width), BF16),
            pltpu.VMEM((span, share), BF16),
            pltpu.VMEM((width, local), BF16),
            pltpu.VMEM((width, local), BF16),
            pltpu.VMEM((width, local), BF16),
            pltpu.VMEM((local, share), BF16),
            pltpu.VMEM((local, share), BF16),
            pltpu.VMEM((span, width), BF16),
            pltpu.VMEM((span, width), BF16),
            pltpu.VMEM((SINK, width), BF16),
            pltpu.VMEM((span, local), BF16),
            pltpu.VMEM((keys, local), BF16),
            pltpu.VMEM((keys, local), BF16),
            pltpu.VMEM((span, TILE), BF16),
            pltpu.VMEM((keys, TILE), BF16),
            pltpu.VMEM((span, TILE), BF16),
            pltpu.VMEM((blocks * 16, TILE), BF16),
            pltpu.VMEM((blocks * 16, TILE), BF16),
            pltpu.VMEM((span, TILE), BF16),
            pltpu.VMEM((span, local), BF16),
            pltpu.VMEM((span, local), BF16),
            pltpu.VMEM((blocks, TILE, TILE), F32),
            pltpu.VMEM((span, local), BF16),
            pltpu.VMEM((blocks, TILE, TILE), F32),
            pltpu.VMEM((span, local), F32),
            pltpu.VMEM((span, local), F32),
            pltpu.VMEM((span, local), F32),
            pltpu.VMEM((blocks, TILE, share), BF16),
            pltpu.VMEM((blocks, TILE, share), BF16),
            pltpu.VMEM((span, share), F32),
            dma((8,)),
            dma((DIRECT,)),
            dma((relays,)),
            dma((chunks,)),
            dma((4 * PIECES,)),
            dma((2 * PIECES,)),
            dma((blocks,)),
            dma((blocks,)),
            dma((1,)),
            dma((1,)),
            dma((blocks,)),
            dma((blocks,)),
            dma((blocks,)),
            dma((blocks,)),
            dma((blocks,)),
            dma((blocks,)),
        ],
        compiler_params=pltpu.CompilerParams(
            collective_id=0, has_side_effects=True, vmem_limit_bytes=60 * 1024 * 1024
        ),
        name="layer",
    )(
        tokens,
        query_weight,
        key_weight,
        value_weight,
        out_weight,
        block_mask[0],
        frame_level,
        modulation,
    )


def solution(mesh):
    placed = (
        P(("batch", "frame"), None),
        P(None, "head"),
        P(None, "head"),
        P(None, "head"),
        P("head", None),
        P(("batch", "frame"), None, None),
        P(("batch", "frame")),
        P(),
    )
    return jax.shard_map(
        shards, mesh=mesh, in_specs=placed, out_specs=P(("batch", "frame"), "head"), check_vma=False
    )
```
